256 devices in a mesh: row: 64 (over z_hi, y, x, core), col: 4 (over z_lo).
Axes of the slice: x: 4, y: 4, z: 8 (z_hi: 2, z_lo: 4; z = z_hi * 4 + z_lo), core: 2. Of those that a mesh axis runs over, the one named last changes fastest.
Arguments:
- node_features: bfloat16 [262144, 256], P(('row', 'col')), may hold values from -6 to 6
- tile_cols: int32 [4096, 8], P(('row', 'col')), may hold values from 0 to 4095, as said below
- tile_weights: int32 [4096, 64, 512], P(('row', 'col')), may hold values from 0 to 7
- w_self: bfloat16 [256, 1024], replicated, may hold values from -0.375 to 0.375
- w_neigh: bfloat16 [256, 1024], replicated, may hold values from -0.375 to 0.375
- bias_hidden: float32 [1024], replicated, may hold values from -3 to 3
- w_out: bfloat16 [1024, 256], replicated, may hold values from -0.1875 to 0.1875
- bias_out: float32 [256], replicated, may hold values from -3 to 3
- cotangent: bfloat16 [262144, 256], P(('row', 'col')), may hold values from -6 to 6
Outputs:
- embed: bfloat16 [262144, 256], P(('row', 'col'))
- grad_features: bfloat16 [262144, 256], P(('row', 'col'))
- grad_w_self: float32 [256, 1024], replicated
- grad_w_neigh: float32 [256, 1024], replicated
- grad_bias_hidden: float32 [1024], replicated
- grad_w_out: float32 [1024, 256], replicated
- grad_bias_out: float32 [256], replicated
The draws below stay inside these ranges and needn't reach their ends.
Inputs may be any that keep to these rules, and one draw needn't show every extreme that they name: `tile_cols`: the first tile of block row b is its diagonal block b. The second lies exactly 16 block rows before or after b (the side drawn for each row), clipped to the graph. Every tile's block column differs from its block row by at most 16.
All inputs are finite; a program needn't handle non-finite values.
Results may differ from the reference program's by a relative error of at most 0.0071.
Values may be sent and summed in bfloat16 or wider, within the bound.
A program may use at most 128 MiB of HBM per device.

```python
import math
import jax
import jax.numpy as jnp
from jax import lax

F = 256
HID = 1024
TILE = 64
TPB = 8
CH = 1024
CB = 16
NB = 4096
NODES = 262144


def draw_tile_cols(key, part):
    first_key, second_key = jax.random.split(key, 2)
    block_index = jnp.arange(NB, dtype=jnp.int32)[:, None]
    slot_index = jnp.arange(TPB, dtype=jnp.int32)[None, :]
    offsets = jax.random.randint(first_key, (NB, TPB), -CB, CB + 1, dtype=jnp.int32)
    sides = jax.random.randint(second_key, (NB, 1), 0, 2, dtype=jnp.int32) * 2 - 1
    offsets = jnp.where(slot_index == 0, 0, jnp.where(slot_index == 1, sides * CB, offsets))
    return jnp.clip(block_index + offsets, 0, NB - 1).astype(jnp.int32)


def plant(array, own_key, low, largest):
    shape = array.shape
    spot = [jax.random.randint(jax.random.fold_in(own_key, axis), (), 0, shape[axis]) for axis in range(len(shape))]
    array = array.at[tuple(spot)].set(low)
    longest = shape.index(max(shape))
    spot[longest] = (spot[longest] + 1) % shape[longest]
    return array.at[tuple(spot)].set(largest)


def level_of(own_key, dims, cuts, low, top_value):
    loudness, own = 1.0, jax.random.fold_in(own_key, 6)
    for position, parts in cuts:
        draws = jnp.exp(jax.random.uniform(jax.random.fold_in(own, position), (parts,), jnp.float32, low / len(cuts), top_value / len(cuts)))
        loudness = loudness * jnp.repeat(draws, dims[position] // parts).reshape([-1 if axis == position else 1 for axis in range(len(dims))])
    return loudness


def bell_draw(own_key, dims, scale, bound, cuts=(), kind=jnp.bfloat16):
    array = jax.random.normal(own_key, dims, jnp.float32) * scale
    if len(cuts) > 0:
        array = level_of(own_key, dims, cuts, -0.22, 0.18) * array
    return jnp.clip(array, min=-bound, max=bound).astype(kind)


def setup_inputs(seed: int = 0) -> dict:
    keys = jax.random.split(jax.random.key(seed), 10)
    node_features = bell_draw(keys[0], (NODES, F), 1.0, 6.0, ((0, 256),))
    tile_cols = draw_tile_cols(jax.random.fold_in(keys[9], 71), 0)
    tile_weights = plant(jax.random.randint(keys[2], (NB, TILE, TPB * TILE), 0, 8), jax.random.fold_in(keys[2], 1), 0, 7).astype(jnp.int32)
    w_self = bell_draw(keys[3], (F, HID), F ** -0.5, 0.375)
    w_neigh = bell_draw(keys[4], (F, HID), F ** -0.5, 0.375)
    bias_hidden = bell_draw(keys[5], (HID,), 0.5, 3.0, (), jnp.float32)
    w_out = bell_draw(keys[6], (HID, F), HID ** -0.5, 0.1875)
    bias_out = bell_draw(keys[7], (F,), 0.5, 3.0, (), jnp.float32)
    cotangent = bell_draw(keys[8], (NODES, F), 1.0, 6.0, ((0, 256),))
    return {"node_features": node_features, "tile_cols": tile_cols, "tile_weights": tile_weights, "w_self": w_self, "w_neigh": w_neigh, "bias_hidden": bias_hidden, "w_out": w_out, "bias_out": bias_out, "cotangent": cotangent}


def gelu_tanh(values):
    return jax.nn.gelu(values, approximate=True)

def reference(node_features, tile_cols, tile_weights, w_self, w_neigh, bias_hidden, w_out, bias_out, cotangent):
    tile_scale = 0.25 / math.sqrt(TPB * TILE)
    groups = NB // CB
    all_blocks = node_features.reshape(NB, TILE, F)
    group_inputs = (node_features.reshape(groups, CH, F), tile_cols.reshape(groups, CB, TPB), tile_weights.reshape(groups, CB, TILE, TPB * TILE), cotangent.reshape(groups, CH, F))

    def advance(state_pair, inputs):
        partials, adjoint_sum = state_pair
        features, columns, weights, incoming = inputs
        adjacency = (weights.astype(jnp.float32) * tile_scale).astype(jnp.bfloat16)
        gathered = all_blocks[columns].reshape(CB, TPB * TILE, F)
        aggregate = jnp.einsum('bij,bjf->bif', adjacency.astype(jnp.float32), gathered.astype(jnp.float32))
        aggregate = aggregate.reshape(CH, F).astype(jnp.bfloat16)
        preact = jnp.dot(features, w_self, preferred_element_type=jnp.float32) + jnp.dot(aggregate, w_neigh, preferred_element_type=jnp.float32) + bias_hidden
        activated, pullback = jax.vjp(gelu_tanh, preact)
        hidden = activated.astype(jnp.bfloat16)
        embed_rows = (jnp.dot(hidden, w_out, preferred_element_type=jnp.float32) + bias_out).astype(jnp.bfloat16)
        d_act = jnp.dot(incoming, w_out.T, preferred_element_type=jnp.float32)
        d_hidden = pullback(d_act)[0].astype(jnp.bfloat16)
        partials = (partials[0] + jnp.dot(features.T, d_hidden, preferred_element_type=jnp.float32), partials[1] + jnp.dot(aggregate.T, d_hidden, preferred_element_type=jnp.float32), partials[2] + lax.optimization_barrier(jnp.sum(d_hidden.astype(jnp.float32), axis=0)), partials[3] + jnp.dot(hidden.T, incoming, preferred_element_type=jnp.float32), partials[4] + lax.optimization_barrier(jnp.sum(incoming.astype(jnp.float32), axis=0)))
        d_aggregate = jnp.dot(d_hidden, w_neigh.T, preferred_element_type=jnp.float32).astype(jnp.bfloat16)
        d_self = jnp.dot(d_hidden, w_self.T, preferred_element_type=jnp.float32)
        spread = jnp.einsum('bij,bif->bjf', adjacency.astype(jnp.float32), d_aggregate.reshape(CB, TILE, F).astype(jnp.float32))
        spread = spread.reshape(CB * TPB, TILE, F)
        adjoint_sum = adjoint_sum.at[columns.reshape(-1)].add(spread)
        return ((partials, adjoint_sum), (embed_rows, d_self))
    start_partials = (jnp.zeros((F, HID), jnp.float32), jnp.zeros((F, HID), jnp.float32), jnp.zeros((HID,), jnp.float32), jnp.zeros((HID, F), jnp.float32), jnp.zeros((F,), jnp.float32))
    start_adjoint = jnp.zeros((NB, TILE, F), jnp.float32)
    (partials, adjoint_sum), (embed_rows, d_self) = lax.scan(advance, (start_partials, start_adjoint), group_inputs)
    embed = embed_rows.reshape(NODES, F)
    grad_features = (d_self.reshape(NODES, F) + adjoint_sum.reshape(NODES, F)).astype(jnp.bfloat16)
    grad_scale = 1.0 / math.sqrt(NODES)
    return (embed, grad_features, partials[0] * grad_scale, partials[1] * grad_scale, partials[2] * grad_scale, partials[3] * grad_scale, partials[4] * grad_scale)
```

```python
import functools, math
import jax, jax.numpy as jnp
from jax import lax
from jax.experimental import pallas as pl
from jax.experimental.pallas import tpu as pltpu
from jax.sharding import PartitionSpec as P

MESH = pl.DeviceIdType.MESH
BF, F32 = jnp.bfloat16, jnp.float32


def coords():
    row, z_lo = lax.axis_index("row"), lax.axis_index("col")
    core = row % 2
    x = (row // 2) % 4
    y = (row // 8) % 4
    z = (row // 32) * 4 + z_lo
    return row, z_lo, core, x, y, z


def partners():
    row, z_lo, core, x, y, z = coords()
    sibling = [(row + 1 - 2 * core, z_lo, 1 - core)]
    xs = [(row + ((x + d) % 4 - x) * 2, z_lo, (x + d) % 4) for d in (2, 1, 3)]
    ys = [(row + ((y + d) % 4 - y) * 8, z_lo, (y + d) % 4) for d in (2, 1, 3)]
    zs = []
    for d in (4, 3, 5, 2, 6, 1, 7):
        k = (z + d) % 8
        zs.append((row + (k // 4 - z // 4) * 32, k % 4, k))
    return sibling, xs, ys, zs


def remote(src, dst, send, recv, dev):
    return pltpu.make_async_remote_copy(
        src_ref=src, dst_ref=dst, send_sem=send, recv_sem=recv,
        device_id=(dev[0], dev[1]), device_id_type=MESH)


def reduce_all(g, bias, gout, bout, rc, s1, r1, t1, r2, zin, rz, zc, zfull, bc, bx, by, bz,
               send, recv):
    row, z_lo, core, x, y, z = coords()
    sibling, xs, ys, zs = partners()
    A, B = 384, 96
    sent = []
    nsend = [0]

    def go(src, dst, rsem, dev):
        c = remote(src, dst, send.at[nsend[0]], recv.at[rsem], dev)
        nsend[0] += 1
        c.start()
        sent.append(c)

    def land(dst, rsem):
        remote(dst, dst, send.at[0], recv.at[rsem], sibling[0]).wait_recv()

    mine = pl.ds(pl.multiple_of(core * 512, 512), 512)
    other = pl.ds(pl.multiple_of((1 - core) * 512, 512), 512)
    go(g.at[:, other], rc, 0, sibling[0])
    go(bias, bc, 1, sibling[0])
    land(rc, 0)
    land(bc, 1)

    @pl.loop(0, 8)
    def _(i):
        rows = pl.ds(pl.multiple_of(i * 96, 96), 96)
        s1[rows, :] = (g[rows, mine].astype(F32) + rc[rows, :].astype(F32)).astype(BF)

    b1 = bias[...] + bc[...]
    bx[x] = b1
    base = 2
    for h, (line, me) in enumerate(((xs, x), (ys, y))):
        for dev in line:
            j = dev[2]
            rows = pl.ds(pl.multiple_of(h * A + j * B, B), B)
            go(s1.at[rows, :], r1.at[h, me], base + h * 4 + me, dev)
    for dev in xs:
        go(bx.at[x], bx.at[x], base + 8 + x, dev)
    for h, (line, me) in enumerate(((xs, x), (ys, y))):
        for dev in line:
            land(r1.at[h, dev[2]], base + h * 4 + dev[2])
        own = pl.ds(pl.multiple_of(h * A + me * B, B), B)
        total = s1[own, :].astype(F32)
        for dev in line:
            total = total + r1[h, dev[2]].astype(F32)
        t1[h] = total.astype(BF)
    for dev in xs:
        land(bx.at[dev[2]], base + 8 + dev[2])
    by[y] = bx[0] + bx[1] + bx[2] + bx[3]
    base = 14
    for h, (line, me) in enumerate(((ys, y), (xs, x))):
        for dev in line:
            lanes = pl.ds(pl.multiple_of(dev[2] * 128, 128), 128)
            go(t1.at[h, :, lanes], r2.at[h, me], base + h * 4 + me, dev)
    for dev in ys:
        go(by.at[y], by.at[y], base + 8 + y, dev)
    for h, (line, me) in enumerate(((ys, y), (xs, x))):
        for dev in line:
            land(r2.at[h, dev[2]], base + h * 4 + dev[2])
        total = t1[h, :, pl.ds(pl.multiple_of(me * 128, 128), 128)].astype(F32)
        for dev in line:
            total = total + r2[h, dev[2]].astype(F32)
        zin[h * 4 : h * 4 + 4] = total.reshape(4, 24, 128)
    for dev in ys:
        land(by.at[dev[2]], base + 8 + dev[2])
    bz[z] = by[0] + by[1] + by[2] + by[3]
    base = 26
    for dev in zs:
        go(zin.at[dev[2]], rz.at[z], base + z, dev)
    for dev in zs:
        go(bz.at[z], bz.at[z], base + 8 + z, dev)
    total = zin[z]
    for dev in zs:
        land(rz.at[dev[2]], base + dev[2])
        total = total + rz[dev[2]]
    zfull[z] = total
    base = 42
    for dev in zs:
        go(zfull.at[z], zfull.at[z], base + z, dev)
    for dev in zs:
        land(bz.at[dev[2]], 34 + dev[2])
    bout[...] = (((bz[0] + bz[1]) + (bz[2] + bz[3])) + ((bz[4] + bz[5]) + (bz[6] + bz[7])))
    for dev in zs:
        land(zfull.at[dev[2]], base + dev[2])
    base = 50
    for h, (own, line, me) in enumerate(((x, ys, y), (y, xs, x))):
        rows = pl.ds(pl.multiple_of(h * A + own * B, B), B)
        lane0 = core * 512

        def at(j):
            return pl.ds(pl.multiple_of(lane0 + j * 128, 128), 128)

        gout[rows, at(me)] = zfull[h * 4 : h * 4 + 4].reshape(96, 128).astype(BF)
        for dev in line:
            go(gout.at[rows, at(me)], gout.at[rows, at(me)], base + h * 4 + me, dev)
    for h, (own, line, me) in enumerate(((x, ys, y), (y, xs, x))):
        rows = pl.ds(pl.multiple_of(h * A + own * B, B), B)
        lane0 = core * 512
        for dev in line:
            piece = gout.at[rows, pl.ds(pl.multiple_of(lane0 + dev[2] * 128, 128), 128)]
            land(piece, base + h * 4 + dev[2])
    base = 58
    for h, (line, me) in enumerate(((xs, x), (ys, y))):
        rows = pl.ds(pl.multiple_of(h * A + me * B, B), B)
        for dev in line:
            go(gout.at[rows, mine], gout.at[rows, mine], base + h * 4 + me, dev)
        go(gout.at[rows, mine], gout.at[rows, mine], 66 + h * 4 + me, sibling[0])
    for h, (line, me) in enumerate(((xs, x), (ys, y))):
        for dev in line:
            rows = pl.ds(pl.multiple_of(h * A + dev[2] * B, B), B)
            land(gout.at[rows, mine], base + h * 4 + dev[2])
            go(gout.at[rows, mine], gout.at[rows, mine], 66 + h * 4 + dev[2], sibling[0])
    for h in range(2):
        for j in range(4):
            rows = pl.ds(h * A + j * B, B)
            land(gout.at[rows, other], 66 + h * 4 + j)
    for c in sent:
        c.wait_send()


AR_SCRATCH = [
    pltpu.VMEM((768, 512), BF),
    pltpu.VMEM((768, 512), BF),
    pltpu.VMEM((2, 4, 96, 512), BF),
    pltpu.VMEM((2, 96, 512), BF),
    pltpu.VMEM((2, 4, 96, 128), BF),
    pltpu.VMEM((8, 24, 128), F32),
    pltpu.VMEM((8, 24, 128), F32),
    pltpu.VMEM((24, 128), F32),
    pltpu.VMEM((8, 24, 128), F32),
    pltpu.VMEM((16, 128), F32),
    pltpu.VMEM((4, 16, 128), F32),
    pltpu.VMEM((4, 16, 128), F32),
    pltpu.VMEM((8, 16, 128), F32),
    pltpu.SemaphoreType.DMA((80,)),
    pltpu.SemaphoreType.DMA((80,)),
]


def greet(devs):
    barrier = pltpu.get_barrier_semaphore()
    for dev in devs:
        pl.semaphore_signal(barrier, inc=1, device_id=(dev[0], dev[1]), device_id_type=MESH)
    pl.semaphore_wait(barrier, len(devs))


def ar_kernel(g, bias, gout, bout, *scratch):
    sibling, xs, ys, zs = partners()
    greet(sibling + xs + ys + zs)
    reduce_all(g, bias, gout, bout, *scratch)


def all_reduce(g, bias):
    vm = pl.BlockSpec(memory_space=pltpu.VMEM)
    return pl.pallas_call(
        ar_kernel,
        out_shape=(jax.ShapeDtypeStruct((768, 1024), BF), jax.ShapeDtypeStruct((16, 128), F32)),
        in_specs=[vm, vm], out_specs=(vm, vm), scratch_shapes=AR_SCRATCH,
        compiler_params=pltpu.CompilerParams(collective_id=0, has_side_effects=True,
                                             vmem_limit_bytes=32 << 20),
        name="reduce_grads",
    )(g, bias)


def extended(block, sides, width):
    for axis, dim in sides:
        count = lax.axis_size(axis)
        forward = [(i, i + 1) for i in range(count - 1)]
        backward = [(target, source) for source, target in forward]
        low = lax.ppermute(
            lax.slice_in_dim(block, block.shape[dim] - width, None, axis=dim), axis, forward
        )
        high = lax.ppermute(lax.slice_in_dim(block, 0, width, axis=dim), axis, backward)
        block = jnp.concatenate([low, block, high], axis=dim)
    return block


def gelu_tanh(values):
    return jax.nn.gelu(values, approximate=True)


def reduce_grads(partials):
    g = jnp.concatenate([partials[0], partials[1], partials[3]], axis=0).astype(BF)
    bias = jnp.concatenate(
        [partials[2], partials[4], jnp.zeros((768,), F32)]).reshape(16, 128)
    g, bias = all_reduce(g, bias)
    g = g.astype(F32)
    bias = bias.reshape(-1)
    return g[:256], g[256:512], bias[:1024], g[512:].T, bias[1024:1280]


def adjoint_part(adjacency, d_aggregate, local_idx, block_rows, tile_size, per_row, width):
    rows_here = block_rows * tile_size
    spread = jnp.einsum(
        "bij,bif->bjf",
        adjacency,
        d_aggregate.reshape(block_rows, tile_size, width),
        preferred_element_type=jnp.float32,
    )
    spread = spread.reshape(block_rows * per_row, tile_size, width)
    spread_sum = jnp.zeros((3 * block_rows, tile_size, width), jnp.float32)
    spread_sum = spread_sum.at[local_idx.reshape(-1)].add(spread)
    spread_sum = spread_sum.reshape(3 * rows_here, width)
    outer_parts = jnp.concatenate([spread_sum[:rows_here], spread_sum[2 * rows_here :]], axis=0)
    padded = extended(outer_parts, ((("row", "col"), 0),), rows_here)
    return spread_sum[rows_here : 2 * rows_here] + padded[:rows_here] + padded[3 * rows_here :]


def local(
    node_features, tile_cols, tile_weights, w_self, w_neigh, bias_hidden, w_out, bias_out, cotangent
):
    rows_here = node_features.shape[0]
    width = node_features.shape[1]
    tile_size = tile_weights.shape[1]
    per_row = tile_cols.shape[1]
    block_rows = rows_here // tile_size
    devices_all = lax.axis_size(("row", "col"))
    tile_scale = 0.25 / math.sqrt(per_row * tile_size)
    grad_scale = 1.0 / math.sqrt(rows_here * devices_all)
    window = extended(node_features, ((("row", "col"), 0),), rows_here)
    first_block = lax.axis_index(("row", "col")) * block_rows - block_rows
    local_idx = tile_cols - first_block
    all_blocks = window.reshape(3 * block_rows, tile_size, width)
    gathered = all_blocks[local_idx].reshape(block_rows, per_row * tile_size, width)
    adjacency = (tile_weights.astype(jnp.float32) * tile_scale).astype(jnp.bfloat16)
    aggregate = jnp.einsum("bij,bjf->bif", adjacency, gathered, preferred_element_type=jnp.float32)
    aggregate = aggregate.reshape(rows_here, width).astype(jnp.bfloat16)
    preact = (
        jnp.dot(node_features, w_self, preferred_element_type=jnp.float32)
        + jnp.dot(aggregate, w_neigh, preferred_element_type=jnp.float32)
        + bias_hidden
    )
    activated, pullback = jax.vjp(gelu_tanh, preact)
    hidden = activated.astype(jnp.bfloat16)
    embed = (jnp.dot(hidden, w_out, preferred_element_type=jnp.float32) + bias_out).astype(
        jnp.bfloat16
    )
    d_act = jnp.dot(cotangent, w_out.T, preferred_element_type=jnp.float32)
    d_hidden = pullback(d_act)[0].astype(jnp.bfloat16)
    partials = (
        jnp.dot(node_features.T, d_hidden, preferred_element_type=jnp.float32),
        jnp.dot(aggregate.T, d_hidden, preferred_element_type=jnp.float32),
        jnp.sum(d_hidden.astype(jnp.float32), axis=0),
        jnp.dot(cotangent.T, hidden, preferred_element_type=jnp.float32),
        jnp.sum(cotangent.astype(jnp.float32), axis=0),
    )
    d_aggregate = jnp.dot(d_hidden, w_neigh.T, preferred_element_type=jnp.float32).astype(
        jnp.bfloat16
    )
    d_self = jnp.dot(d_hidden, w_self.T, preferred_element_type=jnp.float32)
    rim_total = adjoint_part(
        adjacency, d_aggregate, local_idx, block_rows, tile_size, per_row, width
    )
    reduced = reduce_grads(partials)
    grad_features = (d_self + rim_total).astype(jnp.bfloat16)
    return (
        embed,
        grad_features,
        reduced[0] * grad_scale,
        reduced[1] * grad_scale,
        reduced[2] * grad_scale,
        reduced[3] * grad_scale,
        reduced[4] * grad_scale,
    )


def solution(mesh):
    in_specs = (
        P(("row", "col"), None),
        P(("row", "col"), None),
        P(("row", "col"), None, None),
        P(),
        P(),
        P(),
        P(),
        P(),
        P(("row", "col"), None),
    )
    out_specs = (P(("row", "col"), None), P(("row", "col"), None), P(), P(), P(), P(), P())
    return jax.shard_map(local, mesh=mesh, in_specs=in_specs, out_specs=out_specs, check_vma=False)
```

```python
import math

import jax
import jax.numpy as jnp
from jax import lax
from jax.experimental import pallas as pl
from jax.experimental.pallas import tpu as pltpu
from jax.sharding import PartitionSpec as P

MESH = pl.DeviceIdType.MESH
BF, F32 = jnp.bfloat16, jnp.float32


def coords():
    row, z_lo = lax.axis_index("row"), lax.axis_index("col")
    core = row % 2
    x = (row // 2) % 4
    y = (row // 8) % 4
    z = (row // 32) * 4 + z_lo
    return row, z_lo, core, x, y, z


def partners():
    row, z_lo, core, x, y, z = coords()
    sibling = [(row + 1 - 2 * core, z_lo, 1 - core)]
    xs = [(row + ((x + d) % 4 - x) * 2, z_lo, (x + d) % 4) for d in (2, 1, 3)]
    ys = [(row + ((y + d) % 4 - y) * 8, z_lo, (y + d) % 4) for d in (2, 1, 3)]
    zs = []
    for d in (4, 3, 5, 2, 6, 1, 7):
        k = (z + d) % 8
        zs.append((row + (k // 4 - z // 4) * 32, k % 4, k))
    return sibling, xs, ys, zs


def remote(src, dst, send, recv, dev):
    return pltpu.make_async_remote_copy(
        src_ref=src, dst_ref=dst, send_sem=send, recv_sem=recv,
        device_id=(dev[0], dev[1]), device_id_type=MESH)


def reduce_all(g, bias, gout, bout, rc, s1, r1, t1, r2, zin, rz, zc, zfull, bc, bx, by, bz,
               send, recv, hook=None):
    row, z_lo, core, x, y, z = coords()
    sibling, xs, ys, zs = partners()
    A, B = 384, 96
    sent = []
    nsend = [0]

    def go(src, dst, rsem, dev):
        c = remote(src, dst, send.at[nsend[0]], recv.at[rsem], dev)
        nsend[0] += 1
        c.start()
        sent.append(c)

    def land(dst, rsem):
        remote(dst, dst, send.at[0], recv.at[rsem], sibling[0]).wait_recv()

    mine = pl.ds(pl.multiple_of(core * 512, 512), 512)
    other = pl.ds(pl.multiple_of((1 - core) * 512, 512), 512)
    go(g.at[:, other], rc, 0, sibling[0])
    go(bias, bc, 1, sibling[0])
    if hook is not None:
        hook()
    land(rc, 0)
    land(bc, 1)

    @pl.loop(0, 8)
    def _(i):
        rows = pl.ds(pl.multiple_of(i * 96, 96), 96)
        s1[rows, :] = (g[rows, mine].astype(F32) + rc[rows, :].astype(F32)).astype(BF)

    b1 = bias[...] + bc[...]
    bx[x] = b1
    base = 2
    for h, (line, me) in enumerate(((xs, x), (ys, y))):
        for dev in line:
            j = dev[2]
            rows = pl.ds(pl.multiple_of(h * A + j * B, B), B)
            go(s1.at[rows, :], r1.at[h, me], base + h * 4 + me, dev)
    for dev in xs:
        go(bx.at[x], bx.at[x], base + 8 + x, dev)
    for h, (line, me) in enumerate(((xs, x), (ys, y))):
        for dev in line:
            land(r1.at[h, dev[2]], base + h * 4 + dev[2])
        own = pl.ds(pl.multiple_of(h * A + me * B, B), B)
        total = s1[own, :].astype(F32)
        for dev in line:
            total = total + r1[h, dev[2]].astype(F32)
        t1[h] = total.astype(BF)
    for dev in xs:
        land(bx.at[dev[2]], base + 8 + dev[2])
    by[y] = bx[0] + bx[1] + bx[2] + bx[3]
    base = 14
    for h, (line, me) in enumerate(((ys, y), (xs, x))):
        for dev in line:
            lanes = pl.ds(pl.multiple_of(dev[2] * 128, 128), 128)
            go(t1.at[h, :, lanes], r2.at[h, me], base + h * 4 + me, dev)
    for dev in ys:
        go(by.at[y], by.at[y], base + 8 + y, dev)
    for h, (line, me) in enumerate(((ys, y), (xs, x))):
        for dev in line:
            land(r2.at[h, dev[2]], base + h * 4 + dev[2])
        total = t1[h, :, pl.ds(pl.multiple_of(me * 128, 128), 128)].astype(F32)
        for dev in line:
            total = total + r2[h, dev[2]].astype(F32)
        zin[h * 4 : h * 4 + 4] = total.reshape(4, 24, 128)
    for dev in ys:
        land(by.at[dev[2]], base + 8 + dev[2])
    bz[z] = by[0] + by[1] + by[2] + by[3]
    base = 26
    for dev in zs:
        go(zin.at[dev[2]], rz.at[z], base + z, dev)
    for dev in zs:
        go(bz.at[z], bz.at[z], base + 8 + z, dev)
    total = zin[z]
    for dev in zs:
        land(rz.at[dev[2]], base + dev[2])
        total = total + rz[dev[2]]
    zfull[z] = total
    base = 42
    for dev in zs:
        go(zfull.at[z], zfull.at[z], base + z, dev)
    for dev in zs:
        land(bz.at[dev[2]], 34 + dev[2])
    bout[...] = (((bz[0] + bz[1]) + (bz[2] + bz[3])) + ((bz[4] + bz[5]) + (bz[6] + bz[7])))
    for dev in zs:
        land(zfull.at[dev[2]], base + dev[2])
    base = 50
    for h, (own, line, me) in enumerate(((x, ys, y), (y, xs, x))):
        rows = pl.ds(pl.multiple_of(h * A + own * B, B), B)
        lane0 = core * 512

        def at(j):
            return pl.ds(pl.multiple_of(lane0 + j * 128, 128), 128)

        gout[rows, at(me)] = zfull[h * 4 : h * 4 + 4].reshape(96, 128).astype(BF)
        for dev in line:
            go(gout.at[rows, at(me)], gout.at[rows, at(me)], base + h * 4 + me, dev)
    for h, (own, line, me) in enumerate(((x, ys, y), (y, xs, x))):
        rows = pl.ds(pl.multiple_of(h * A + own * B, B), B)
        lane0 = core * 512
        for dev in line:
            piece = gout.at[rows, pl.ds(pl.multiple_of(lane0 + dev[2] * 128, 128), 128)]
            land(piece, base + h * 4 + dev[2])
    base = 58
    for h, (line, me) in enumerate(((xs, x), (ys, y))):
        rows = pl.ds(pl.multiple_of(h * A + me * B, B), B)
        for dev in line:
            go(gout.at[rows, mine], gout.at[rows, mine], base + h * 4 + me, dev)
        go(gout.at[rows, mine], gout.at[rows, mine], 66 + h * 4 + me, sibling[0])
    for h, (line, me) in enumerate(((xs, x), (ys, y))):
        for dev in line:
            rows = pl.ds(pl.multiple_of(h * A + dev[2] * B, B), B)
            land(gout.at[rows, mine], base + h * 4 + dev[2])
            go(gout.at[rows, mine], gout.at[rows, mine], 66 + h * 4 + dev[2], sibling[0])
    for h in range(2):
        for j in range(4):
            rows = pl.ds(h * A + j * B, B)
            land(gout.at[rows, other], 66 + h * 4 + j)
    for c in sent:
        c.wait_send()


AR_SCRATCH = [
    pltpu.VMEM((768, 512), BF),
    pltpu.VMEM((768, 512), BF),
    pltpu.VMEM((2, 4, 96, 512), BF),
    pltpu.VMEM((2, 96, 512), BF),
    pltpu.VMEM((2, 4, 96, 128), BF),
    pltpu.VMEM((8, 24, 128), F32),
    pltpu.VMEM((8, 24, 128), F32),
    pltpu.VMEM((24, 128), F32),
    pltpu.VMEM((8, 24, 128), F32),
    pltpu.VMEM((16, 128), F32),
    pltpu.VMEM((4, 16, 128), F32),
    pltpu.VMEM((4, 16, 128), F32),
    pltpu.VMEM((8, 16, 128), F32),
    pltpu.SemaphoreType.DMA((80,)),
    pltpu.SemaphoreType.DMA((80,)),
]


def greet(devs):
    barrier = pltpu.get_barrier_semaphore()
    for dev in devs:
        pl.semaphore_signal(barrier, inc=1, device_id=(dev[0], dev[1]), device_id_type=MESH)
    pl.semaphore_wait(barrier, len(devs))


SCALE_TILE = 0.25 / math.sqrt(512)
C0 = math.sqrt(2.0 / math.pi)
C1 = C0 * 0.044715
T_RHS = (((1,), (1,)), ((), ()))


def mm(a, b):
    return jnp.dot(a, b, preferred_element_type=F32)


def mm_t(a, b):
    return lax.dot_general(a, b, T_RHS, preferred_element_type=F32)


def ds256(i):
    return pl.ds(pl.multiple_of(i * 256, 256), 256)


def neighbours():
    row, z_lo, core, x, y, z = coords()
    here = row * 4 + z_lo
    right = (here + 1) % 256
    left = (here + 255) % 256
    return here, (left // 4, left % 4), (right // 4, right % 4)


def layer_kernel(
    cols, x_hbm, tw_hbm, ws_hbm, wn_hbm, bh, wo_hbm, bo, cot_hbm,
    embed, gradf, gout, bout,
    win, tw, ws, wn, wo, cot, dup, dense, dense_t, pre, dact, agg0, agg, xt, ct, at,
    hid, dh, dagg, bsum, own, lo, hi, lo_b, hi_b, from_r, from_l, g, bias,
    in_sem, halo_send, halo_recv, *ar,
):
    here, left, right = neighbours()
    sibling, xs, ys, zs = partners()

    loads = []
    for n, (src, dst) in enumerate((
        (tw_hbm, tw), (x_hbm, win.at[pl.ds(1024, 1024), :]), (cot_hbm, cot),
        (ws_hbm, ws), (wo_hbm, wo), (wn_hbm, wn),
    )):
        c = pltpu.make_async_copy(src, dst, in_sem.at[n])
        c.start()
        loads.append(c)
    greet([left, right] + sibling + xs + ys + zs)

    halo = []

    def halo_copy(src, dst, n, dev):
        c = remote(src, dst, halo_send.at[n], halo_recv.at[n], dev)
        c.start()
        halo.append(c)

    for i in range(4):
        far = pl.ds(256 * (3 - i), 256)
        near = pl.ds(256 * i, 256)
        halo_copy(x_hbm.at[far, :], win.at[far, :], 3 - i, right)
        halo_copy(x_hbm.at[near, :], win.at[pl.ds(2048 + 256 * i, 256), :], 4 + i, left)

    def halo_wait(n):
        dst = win.at[pl.ds(256 * n if n < 4 else 1024 + 256 * n, 256), :]
        remote(dst, dst, halo_send.at[n], halo_recv.at[n], left).wait_recv()

    loads[0].wait()
    lane = lax.broadcasted_iota(jnp.int32, (64, 128), 1)
    half = lax.broadcasted_iota(jnp.int32, (1, 128), 1) // 64

    @pl.loop(0, 16)
    def _(p):
        c = p // 4
        rows = pl.ds(pl.multiple_of((p % 4) * 64, 64), 64)
        base = here * 16 - 16 + 4 * c
        for q in range(4):
            u = tw[p, :, 128 * q : 128 * q + 128].astype(F32) * SCALE_TILE
            u = u.astype(BF).astype(F32)
            r = pltpu.roll(u, 64, 1)
            dup[2 * q] = jnp.where(lane < 64, u, r)
            dup[2 * q + 1] = jnp.where(lane < 64, r, u)
        spot = [cols[p, s] - base for s in range(8)]

        @pl.loop(0, 18)
        def _(j):
            total = jnp.zeros((64, 128), F32)
            for s in range(8):
                hit = jnp.where(half == spot[s] - 2 * j, 1.0, 0.0).astype(F32)
                total = total + dup[s] * hit
            dense[c, rows, pl.ds(pl.multiple_of(j * 128, 128), 128)] = total.astype(BF)

    @pl.loop(0, 36)
    def _(i):
        c, t = i // 9, i % 9
        dense_t[c, ds256(t), :] = dense[c, :, ds256(t)].T

    for c in loads[1:]:
        c.wait()

    bsum[...] = jnp.zeros_like(bsum)

    @pl.loop(0, 4)
    def _(c):
        rows = ds256(c)
        mine = pl.ds(pl.multiple_of(1024 + c * 256, 256), 256)
        xc = win[mine, :]
        cc = cot[rows, :]
        xt[:, rows] = xc.T
        ct[:, rows] = cc.T
        bsum[:, 1024:1280] += jnp.sum(cc.astype(F32).reshape(32, 8, 256), axis=0)
        for n in range(4):
            n4 = slice(256 * n, 256 * n + 256)
            pre[rows, n4] = mm(xc, ws[:, n4]) + bh[:, n4]
            dact[rows, n4] = mm_t(cc, wo[n4, :])
        total = jnp.zeros((256, 256), F32)
        for t in range(4):
            total = total + mm(dense[c, :, ds256(4 + t - c)], win[1024 + 256 * t : 1280 + 256 * t, :])
        agg0[rows, :] = total

    lo[...] = jnp.zeros_like(lo)
    hi[...] = jnp.zeros_like(hi)

    def adjoint_send(n, buf, src, dst, dev):
        piece = pl.ds(256 * (n % 4), 256)
        buf[piece, :] = src[piece, :].astype(BF)
        halo_copy(buf.at[piece, :], dst.at[piece, :], 8 + n, dev)

    @pl.loop(0, 4)
    def _(k):
        c = (k + 1) % 3 + 2 * (k // 3)

        @pl.when(k == 0)
        def _():
            for n in (3, 4, 2, 5, 1):
                halo_wait(n)

        @pl.when(k == 1)
        def _():
            halo_wait(6)

        @pl.when(k == 2)
        def _():
            halo_wait(0)

        @pl.when(k == 3)
        def _():
            halo_wait(7)

        rows = ds256(c)
        total = agg0[rows, :]
        for t in range(5):
            w = c + t + 4 * ((c + t) // 4)
            total = total + mm(dense[c, :, ds256(w - c)], win[ds256(w), :])
        ag = total.astype(BF)
        agg[rows, :] = ag
        for n in range(4):
            n4 = slice(256 * n, 256 * n + 256)
            pre[rows, n4] += mm(ag, wn[:, n4])

        @pl.loop(0, 8)
        def _(i):
            r = pl.ds(pl.multiple_of(c * 256 + i * 32, 32), 32)
            for n in range(4):
                n4 = slice(256 * n, 256 * n + 256)
                v = pre[r, n4]
                u = v * v
                th = jnp.tanh(v * (C0 + C1 * u))
                a = 0.5 * th + 0.5
                hid[r, n4] = (v * a).astype(BF)
                slope = a + (0.5 * v) * (1.0 - th * th) * (C0 + (3.0 * C1) * u)
                d = (dact[r, n4] * slope).astype(BF)
                dh[r, n4] = d
                bsum[:, n4] += jnp.sum(d.astype(F32).reshape(4, 8, 256), axis=0)

        da = mm_t(dh[rows, :], wn[...]).astype(BF)
        dagg[rows, :] = da
        for t in range(4):
            @pl.when(c + t < 4)
            def _():
                lo[ds256(c + t), :] += mm(dense_t[c, ds256(t), :], da)

            @pl.when(t <= c)
            def _():
                hi[pl.ds(256 * t, 256), :] += mm(dense_t[c, ds256(8 - c + t), :], da)

    for n in (3, 2, 1, 0):
        adjoint_send(4 + n, hi_b, hi, from_l, right)
        adjoint_send(3 - n, lo_b, lo, from_r, left)

    for c in range(4):
        at[:, 256 * c : 256 * c + 256] = agg[256 * c : 256 * c + 256, :].T
    for n in range(4):
        n4 = slice(256 * n, 256 * n + 256)
        g[0:256, n4] = mm(xt[...], dh[:, n4]).astype(BF)
        g[256:512, n4] = mm(at[...], dh[:, n4]).astype(BF)
        g[512:768, n4] = mm(ct[...], hid[:, n4]).astype(BF)
    sums = jnp.sum(bsum[...], axis=0, keepdims=True)
    for n in range(10):
        bias[n : n + 1, :] = sums[:, 128 * n : 128 * n + 128]
    bias[10:16, :] = jnp.zeros((6, 128), F32)

    def local_rest():
        @pl.loop(0, 4)
        def _(c):
            rows = ds256(c)
            embed[rows, :] = (mm(hid[rows, :], wo[...]) + bo[...]).astype(BF)
            total = mm_t(dh[rows, :], ws[...])
            for b in range(4):
                total = total + mm(dense_t[b, ds256(4 + c - b), :], dagg[256 * b : 256 * b + 256, :])
            own[rows, :] = total

    reduce_all(g, bias, gout, bout, *ar, hook=local_rest)

    for n in (3, 2, 1, 0):
        for m, dst in ((4 + n, from_l), (3 - n, from_r)):
            piece = dst.at[pl.ds(256 * (m % 4), 256), :]
            remote(piece, piece, halo_send.at[8 + m], halo_recv.at[8 + m], left).wait_recv()

    @pl.loop(0, 16)
    def _(i):
        r = pl.ds(pl.multiple_of(i * 64, 64), 64)
        gradf[r, :] = (own[r, :] + from_l[r, :].astype(F32) + from_r[r, :].astype(F32)).astype(BF)

    for c in halo:
        c.wait_send()


LAYER_SCRATCH = [
    pltpu.VMEM((3072, 256), BF),
    pltpu.VMEM((16, 64, 512), jnp.int32),
    pltpu.VMEM((256, 1024), BF),
    pltpu.VMEM((256, 1024), BF),
    pltpu.VMEM((1024, 256), BF),
    pltpu.VMEM((1024, 256), BF),
    pltpu.VMEM((8, 64, 128), F32),
    pltpu.VMEM((4, 256, 2304), BF),
    pltpu.VMEM((4, 2304, 256), BF),
    pltpu.VMEM((1024, 1024), F32),
    pltpu.VMEM((1024, 1024), F32),
    pltpu.VMEM((1024, 256), F32),
    pltpu.VMEM((1024, 256), BF),
    pltpu.VMEM((256, 1024), BF),
    pltpu.VMEM((256, 1024), BF),
    pltpu.VMEM((256, 1024), BF),
    pltpu.VMEM((1024, 1024), BF),
    pltpu.VMEM((1024, 1024), BF),
    pltpu.VMEM((1024, 256), BF),
    pltpu.VMEM((8, 1280), F32),
    pltpu.VMEM((1024, 256), F32),
    pltpu.VMEM((1024, 256), F32),
    pltpu.VMEM((1024, 256), F32),
    pltpu.VMEM((1024, 256), BF),
    pltpu.VMEM((1024, 256), BF),
    pltpu.VMEM((1024, 256), BF),
    pltpu.VMEM((1024, 256), BF),
    pltpu.VMEM((768, 1024), BF),
    pltpu.VMEM((16, 128), F32),
    pltpu.SemaphoreType.DMA((6,)),
    pltpu.SemaphoreType.DMA((16,)),
    pltpu.SemaphoreType.DMA((16,)),
]


def local(
    node_features, tile_cols, tile_weights, w_self, w_neigh, bias_hidden, w_out, bias_out, cotangent
):
    vm = pl.BlockSpec(memory_space=pltpu.VMEM)
    hbm = pl.BlockSpec(memory_space=pl.ANY)
    sm = pl.BlockSpec(memory_space=pltpu.SMEM)
    embed, grad_features, g, bias = pl.pallas_call(
        layer_kernel,
        out_shape=(
            jax.ShapeDtypeStruct((1024, 256), BF),
            jax.ShapeDtypeStruct((1024, 256), BF),
            jax.ShapeDtypeStruct((768, 1024), BF),
            jax.ShapeDtypeStruct((16, 128), F32),
        ),
        in_specs=[sm, hbm, hbm, hbm, hbm, vm, hbm, vm, hbm],
        out_specs=(vm, vm, vm, vm),
        scratch_shapes=LAYER_SCRATCH + AR_SCRATCH,
        compiler_params=pltpu.CompilerParams(
            collective_id=0, has_side_effects=True, vmem_limit_bytes=60 << 20
        ),
        name="layer",
    )(
        tile_cols, node_features, tile_weights, w_self, w_neigh,
        bias_hidden.reshape(1, 1024), w_out, bias_out.reshape(1, 256), cotangent,
    )
    scale = 1.0 / math.sqrt(1024 * 256)
    g = g.astype(F32) * scale
    bias = bias.reshape(-1) * scale
    return (
        embed, grad_features, g[:256], g[256:512], bias[:1024], g[512:].T, bias[1024:1280],
    )


def solution(mesh):
    in_specs = (
        P(("row", "col"), None),
        P(("row", "col"), None),
        P(("row", "col"), None, None),
        P(),
        P(),
        P(),
        P(),
        P(),
        P(("row", "col"), None),
    )
    out_specs = (P(("row", "col"), None), P(("row", "col"), None), P(), P(), P(), P(), P())
    return jax.shard_map(local, mesh=mesh, in_specs=in_specs, out_specs=out_specs, check_vma=False)
```

```python
import math

import jax
import jax.numpy as jnp
from jax import lax
from jax.experimental import pallas as pl
from jax.experimental.pallas import tpu as pltpu
from jax.sharding import PartitionSpec as P

MESH = pl.DeviceIdType.MESH
BF, F32 = jnp.bfloat16, jnp.float32


def coords():
    row, z_lo = lax.axis_index("row"), lax.axis_index("col")
    core = row % 2
    x = (row // 2) % 4
    y = (row // 8) % 4
    z = (row // 32) * 4 + z_lo
    return row, z_lo, core, x, y, z


def partners():
    row, z_lo, core, x, y, z = coords()
    sibling = [(row + 1 - 2 * core, z_lo, 1 - core)]
    xs = [(row + ((x + d) % 4 - x) * 2, z_lo, (x + d) % 4) for d in (2, 1, 3)]
    ys = [(row + ((y + d) % 4 - y) * 8, z_lo, (y + d) % 4) for d in (2, 1, 3)]
    zs = []
    for d in (4, 3, 5, 2, 6, 1, 7):
        k = (z + d) % 8
        zs.append((row + (k // 4 - z // 4) * 32, k % 4, k))
    return sibling, xs, ys, zs


def remote(src, dst, send, recv, dev):
    return pltpu.make_async_remote_copy(
        src_ref=src, dst_ref=dst, send_sem=send, recv_sem=recv,
        device_id=(dev[0], dev[1]), device_id_type=MESH)


def reduce_all(g, bias, gout, bout, rc, s1, r1, t1, r2, zin, rz, zc, zfull, bc, bx, by, bz,
               send, recv, hook=None):
    row, z_lo, core, x, y, z = coords()
    sibling, xs, ys, zs = partners()
    A, B = 384, 96
    sent = []
    nsend = [0]

    def go(src, dst, rsem, dev):
        c = remote(src, dst, send.at[nsend[0]], recv.at[rsem], dev)
        nsend[0] += 1
        c.start()
        sent.append(c)

    def land(dst, rsem):
        remote(dst, dst, send.at[0], recv.at[rsem], sibling[0]).wait_recv()

    mine = pl.ds(pl.multiple_of(core * 512, 512), 512)
    other = pl.ds(pl.multiple_of((1 - core) * 512, 512), 512)
    go(g.at[:, other], rc, 0, sibling[0])
    go(bias, bc, 1, sibling[0])
    if hook is not None:
        hook()
    land(rc, 0)
    land(bc, 1)

    @pl.loop(0, 8)
    def _(i):
        rows = pl.ds(pl.multiple_of(i * 96, 96), 96)
        s1[rows, :] = (g[rows, mine].astype(F32) + rc[rows, :].astype(F32)).astype(BF)

    b1 = bias[...] + bc[...]
    bx[x] = b1
    base = 2
    for h, (line, me) in enumerate(((xs, x), (ys, y))):
        for dev in line:
            j = dev[2]
            rows = pl.ds(pl.multiple_of(h * A + j * B, B), B)
            go(s1.at[rows, :], r1.at[h, me], base + h * 4 + me, dev)
    for dev in xs:
        go(bx.at[x], bx.at[x], base + 8 + x, dev)
    for h, (line, me) in enumerate(((xs, x), (ys, y))):
        for dev in line:
            land(r1.at[h, dev[2]], base + h * 4 + dev[2])
        own = pl.ds(pl.multiple_of(h * A + me * B, B), B)
        total = s1[own, :].astype(F32)
        for dev in line:
            total = total + r1[h, dev[2]].astype(F32)
        t1[h] = total.astype(BF)
    for dev in xs:
        land(bx.at[dev[2]], base + 8 + dev[2])
    by[y] = bx[0] + bx[1] + bx[2] + bx[3]
    base = 14
    for h, (line, me) in enumerate(((ys, y), (xs, x))):
        for dev in line:
            lanes = pl.ds(pl.multiple_of(dev[2] * 128, 128), 128)
            go(t1.at[h, :, lanes], r2.at[h, me], base + h * 4 + me, dev)
    for dev in ys:
        go(by.at[y], by.at[y], base + 8 + y, dev)
    for h, (line, me) in enumerate(((ys, y), (xs, x))):
        for dev in line:
            land(r2.at[h, dev[2]], base + h * 4 + dev[2])
        total = t1[h, :, pl.ds(pl.multiple_of(me * 128, 128), 128)].astype(F32)
        for dev in line:
            total = total + r2[h, dev[2]].astype(F32)
        zin[h * 4 : h * 4 + 4] = total.reshape(4, 24, 128)
    for dev in ys:
        land(by.at[dev[2]], base + 8 + dev[2])
    bz[z] = by[0] + by[1] + by[2] + by[3]
    base = 26
    for dev in zs:
        go(zin.at[dev[2]], rz.at[z], base + z, dev)
    for dev in zs:
        go(bz.at[z], bz.at[z], base + 8 + z, dev)
    total = zin[z]
    for dev in zs:
        land(rz.at[dev[2]], base + dev[2])
        total = total + rz[dev[2]]
    zfull[z] = total
    base = 42
    for dev in zs:
        go(zfull.at[z], zfull.at[z], base + z, dev)
    for dev in zs:
        land(bz.at[dev[2]], 34 + dev[2])
    bout[...] = (((bz[0] + bz[1]) + (bz[2] + bz[3])) + ((bz[4] + bz[5]) + (bz[6] + bz[7])))
    for dev in zs:
        land(zfull.at[dev[2]], base + dev[2])
    base = 50
    for h, (own, line, me) in enumerate(((x, ys, y), (y, xs, x))):
        rows = pl.ds(pl.multiple_of(h * A + own * B, B), B)
        lane0 = core * 512

        def at(j):
            return pl.ds(pl.multiple_of(lane0 + j * 128, 128), 128)

        gout[rows, at(me)] = zfull[h * 4 : h * 4 + 4].reshape(96, 128).astype(BF)
        for dev in line:
            go(gout.at[rows, at(me)], gout.at[rows, at(me)], base + h * 4 + me, dev)
    for h, (own, line, me) in enumerate(((x, ys, y), (y, xs, x))):
        rows = pl.ds(pl.multiple_of(h * A + own * B, B), B)
        lane0 = core * 512
        for dev in line:
            piece = gout.at[rows, pl.ds(pl.multiple_of(lane0 + dev[2] * 128, 128), 128)]
            land(piece, base + h * 4 + dev[2])
    base = 58
    for h, (line, me) in enumerate(((xs, x), (ys, y))):
        rows = pl.ds(pl.multiple_of(h * A + me * B, B), B)
        for dev in line:
            go(gout.at[rows, mine], gout.at[rows, mine], base + h * 4 + me, dev)
        go(gout.at[rows, mine], gout.at[rows, mine], 66 + h * 4 + me, sibling[0])
    for h, (line, me) in enumerate(((xs, x), (ys, y))):
        for dev in line:
            rows = pl.ds(pl.multiple_of(h * A + dev[2] * B, B), B)
            land(gout.at[rows, mine], base + h * 4 + dev[2])
            go(gout.at[rows, mine], gout.at[rows, mine], 66 + h * 4 + dev[2], sibling[0])
    for h in range(2):
        for j in range(4):
            rows = pl.ds(h * A + j * B, B)
            land(gout.at[rows, other], 66 + h * 4 + j)
    for c in sent:
        c.wait_send()


AR_SCRATCH = [
    pltpu.VMEM((768, 512), BF),
    pltpu.VMEM((768, 512), BF),
    pltpu.VMEM((2, 4, 96, 512), BF),
    pltpu.VMEM((2, 96, 512), BF),
    pltpu.VMEM((2, 4, 96, 128), BF),
    pltpu.VMEM((8, 24, 128), F32),
    pltpu.VMEM((8, 24, 128), F32),
    pltpu.VMEM((24, 128), F32),
    pltpu.VMEM((8, 24, 128), F32),
    pltpu.VMEM((16, 128), F32),
    pltpu.VMEM((4, 16, 128), F32),
    pltpu.VMEM((4, 16, 128), F32),
    pltpu.VMEM((8, 16, 128), F32),
    pltpu.SemaphoreType.DMA((80,)),
    pltpu.SemaphoreType.DMA((80,)),
]


def greet(devs):
    barrier = pltpu.get_barrier_semaphore()
    for dev in devs:
        pl.semaphore_signal(barrier, inc=1, device_id=(dev[0], dev[1]), device_id_type=MESH)
    pl.semaphore_wait(barrier, len(devs))


SCALE_TILE = 0.25 / math.sqrt(512)
C0 = math.sqrt(2.0 / math.pi)
C1 = C0 * 0.044715
T_RHS = (((1,), (1,)), ((), ()))


def mm(a, b):
    return jnp.dot(a, b, preferred_element_type=F32)


def mm_t(a, b):
    return lax.dot_general(a, b, T_RHS, preferred_element_type=F32)


def ds256(i):
    return pl.ds(pl.multiple_of(i * 256, 256), 256)


def neighbours():
    row, z_lo, core, x, y, z = coords()
    here = row * 4 + z_lo
    right = (here + 1) % 256
    left = (here + 255) % 256
    return here, (left // 4, left % 4), (right // 4, right % 4)


def layer_kernel(
    cols, x_hbm, tw_hbm, ws_hbm, wn_hbm, bh, wo_hbm, bo, cot_hbm,
    embed, gradf, gout, bout,
    win, tw, ws, wn, wo, cot, dup, dense, pre, dact, agg0, xt, ct, at,
    hid, dh, da_t, bsum, own, lo, hi, lo_b, hi_b, from_r, from_l, g, bias,
    in_sem, halo_send, halo_recv, *ar,
):
    here, left, right = neighbours()
    sibling, xs, ys, zs = partners()

    loads = []
    for n, (src, dst) in enumerate((
        (tw_hbm, tw), (x_hbm, win.at[pl.ds(1024, 1024), :]), (cot_hbm, cot),
        (ws_hbm, ws), (wo_hbm, wo), (wn_hbm, wn),
    )):
        c = pltpu.make_async_copy(src, dst, in_sem.at[n])
        c.start()
        loads.append(c)
    greet([left, right] + sibling + xs + ys + zs)

    halo = []

    def halo_copy(src, dst, n, dev):
        c = remote(src, dst, halo_send.at[n], halo_recv.at[n], dev)
        c.start()
        halo.append(c)

    def halo_wait(n):
        dst = win.at[pl.ds(256 * n if n < 4 else 1024 + 256 * n, 256), :]
        remote(dst, dst, halo_send.at[n], halo_recv.at[n], left).wait_recv()

    for i in range(4):
        rows = pl.ds(256 * i, 256)
        halo_copy(x_hbm.at[rows, :], win.at[rows, :], i, right)
    for i in range(4):
        rows = pl.ds(256 * i, 256)
        halo_copy(x_hbm.at[rows, :], win.at[pl.ds(2048 + 256 * i, 256), :], 4 + i, left)

    def build_dense():
        lane = lax.broadcasted_iota(jnp.int32, (64, 128), 1)
        half = lax.broadcasted_iota(jnp.int32, (1, 128), 1) // 64

        @pl.loop(0, 16)
        def _(p):
            c = p // 4
            rows = pl.ds(pl.multiple_of((p % 4) * 64, 64), 64)
            base = here * 16 - 16 + 4 * c
            for q in range(4):
                u = tw[p, :, 128 * q : 128 * q + 128].astype(F32) * SCALE_TILE
                u = u.astype(BF).astype(F32)
                r = pltpu.roll(u, 64, 1)
                dup[2 * q] = jnp.where(lane < 64, u, r)
                dup[2 * q + 1] = jnp.where(lane < 64, r, u)
            spot = [cols[s, p] - base for s in range(8)]

            @pl.loop(0, 18)
            def _(j):
                total = jnp.zeros((64, 128), F32)
                for s in range(8):
                    hit = jnp.where(half == spot[s] - 2 * j, 1.0, 0.0).astype(F32)
                    total = total + dup[s] * hit
                dense[c, rows, pl.ds(pl.multiple_of(j * 128, 128), 128)] = total.astype(BF)

    def local_part():
        bsum[...] = jnp.zeros_like(bsum)

        @pl.loop(0, 4)
        def _(c):
            rows = ds256(c)
            mine = pl.ds(pl.multiple_of(1024 + c * 256, 256), 256)
            xc = win[mine, :]
            cc = cot[rows, :]
            xt[:, rows] = xc.T
            ct[:, rows] = cc.T
            bsum[:, 1024:1280] += jnp.sum(cc.astype(F32).reshape(32, 8, 256), axis=0)
            for n in range(4):
                n4 = slice(256 * n, 256 * n + 256)
                pre[rows, n4] = mm(xc, ws[:, n4]) + bh[:, n4]
                dact[rows, n4] = mm_t(cc, wo[n4, :])
            total = jnp.zeros((256, 256), F32)
            for t in range(4):
                total = total + mm(dense[c, :, ds256(4 + t - c)], win[1024 + 256 * t : 1280 + 256 * t, :])
            agg0[rows, :] = total

    def low_part():
        for c in range(4):
            rows = slice(256 * c, 256 * c + 256)
            total = agg0[rows, :]
            for t in range(c, 4):
                total = total + mm(dense[c, :, 256 * (t - c) : 256 * (t - c) + 256], win[256 * t : 256 * t + 256, :])
            agg0[rows, :] = total

    def adjoint_send(n, buf, src, dst, dev):
        j = n % 4
        buf[j] = src[:, 256 * j : 256 * j + 256].astype(BF)
        halo_copy(buf.at[j], dst.at[j], 8 + n, dev)

    def chunk(c):
        r4 = slice(256 * c, 256 * c + 256)
        total = agg0[r4, :]
        for t in range(c + 1):
            b = 256 * (8 + t - c)
            total = total + mm(dense[c, :, b : b + 256], win[2048 + 256 * t : 2304 + 256 * t, :])
        ag = total.astype(BF)
        for n in range(4):
            n4 = slice(256 * n, 256 * n + 256)
            pre[r4, n4] += mm(ag, wn[:, n4])
        at[:, r4] = ag.T

        @pl.loop(0, 8)
        def _(i):
            r = pl.ds(pl.multiple_of(c * 256 + i * 32, 32), 32)
            for n in range(4):
                n4 = slice(256 * n, 256 * n + 256)
                v = pre[r, n4]
                u = v * v
                a = 0.5 * jnp.tanh(v * (C0 + C1 * u)) + 0.5
                h = v * a
                hid[r, n4] = h.astype(BF)
                slope = a + h * ((2.0 * C0) + (6.0 * C1) * u) * (1.0 - a)
                d = (dact[r, n4] * slope).astype(BF)
                dh[r, n4] = d
                bsum[:, n4] += jnp.sum(d.astype(F32).reshape(4, 8, 256), axis=0)

        da = mm_t(wn[...], dh[r4, :]).astype(BF)
        da_t[c] = da
        for j in range(c, 4):
            part = mm(da, dense[c, :, 256 * (j - c) : 256 * (j - c) + 256])
            j4 = slice(256 * j, 256 * j + 256)
            lo[:, j4] = part if c == 0 else lo[:, j4] + part
            if j == c:
                adjoint_send(j, lo_b, lo, from_r, left)
        for j in range(c + 1):
            b = 256 * (8 + j - c)
            part = mm(da, dense[c, :, b : b + 256])
            j4 = slice(256 * j, 256 * j + 256)
            hi[:, j4] = part if c == j else hi[:, j4] + part
            if c == 3:
                adjoint_send(4 + j, hi_b, hi, from_l, right)

    def weight_grads():
        for n in range(4):
            n4 = slice(256 * n, 256 * n + 256)
            g[0:256, n4] = mm(xt[...], dh[:, n4]).astype(BF)
            g[256:512, n4] = mm(at[...], dh[:, n4]).astype(BF)
            g[512:768, n4] = mm(ct[...], hid[:, n4]).astype(BF)
        sums = jnp.sum(bsum[...], axis=0, keepdims=True)
        for n in range(10):
            bias[n : n + 1, :] = sums[:, 128 * n : 128 * n + 128]
        bias[10:16, :] = jnp.zeros((6, 128), F32)

    def local_rest():
        @pl.loop(0, 4)
        def _(c):
            rows = ds256(c)
            embed[rows, :] = (mm(hid[rows, :], wo[...]) + bo[...]).astype(BF)
            total = jnp.zeros((256, 256), F32)
            for b in range(4):
                total = total + mm(da_t[b], dense[b, :, ds256(4 + c - b)])
            own[rows, :] = mm_t(dh[rows, :], ws[...]) + total.T

    def last_sum():
        for j in (0, 1, 2, 3):
            for m, dst in ((j, from_r), (4 + j, from_l)):
                remote(dst.at[j], dst.at[j], halo_send.at[8 + m], halo_recv.at[8 + m], left).wait_recv()
            rows = slice(256 * j, 256 * j + 256)
            outer = from_l[j].astype(F32) + from_r[j].astype(F32)
            gradf[rows, :] = (own[rows, :] + outer.T).astype(BF)

    loads[0].wait()
    build_dense()
    for c in loads[1:]:
        c.wait()
    local_part()
    for n in range(4):
        halo_wait(n)
    low_part()
    for c in range(4):
        halo_wait(4 + c)
        chunk(c)
    weight_grads()
    reduce_all(g, bias, gout, bout, *ar, hook=local_rest)
    last_sum()
    for c in halo:
        c.wait_send()


LAYER_SCRATCH = [
    pltpu.VMEM((3072, 256), BF),
    pltpu.VMEM((16, 64, 512), jnp.int32),
    pltpu.VMEM((256, 1024), BF),
    pltpu.VMEM((256, 1024), BF),
    pltpu.VMEM((1024, 256), BF),
    pltpu.VMEM((1024, 256), BF),
    pltpu.VMEM((8, 64, 128), F32),
    pltpu.VMEM((4, 256, 2304), BF),
    pltpu.VMEM((1024, 1024), F32),
    pltpu.VMEM((1024, 1024), F32),
    pltpu.VMEM((1024, 256), F32),
    pltpu.VMEM((256, 1024), BF),
    pltpu.VMEM((256, 1024), BF),
    pltpu.VMEM((256, 1024), BF),
    pltpu.VMEM((1024, 1024), BF),
    pltpu.VMEM((1024, 1024), BF),
    pltpu.VMEM((4, 256, 256), BF),
    pltpu.VMEM((8, 1280), F32),
    pltpu.VMEM((1024, 256), F32),
    pltpu.VMEM((256, 1024), F32),
    pltpu.VMEM((256, 1024), F32),
    pltpu.VMEM((4, 256, 256), BF),
    pltpu.VMEM((4, 256, 256), BF),
    pltpu.VMEM((4, 256, 256), BF),
    pltpu.VMEM((4, 256, 256), BF),
    pltpu.VMEM((768, 1024), BF),
    pltpu.VMEM((16, 128), F32),
    pltpu.SemaphoreType.DMA((6,)),
    pltpu.SemaphoreType.DMA((16,)),
    pltpu.SemaphoreType.DMA((16,)),
]


def local(
    node_features, tile_cols, tile_weights, w_self, w_neigh, bias_hidden, w_out, bias_out, cotangent
):
    vm = pl.BlockSpec(memory_space=pltpu.VMEM)
    hbm = pl.BlockSpec(memory_space=pl.ANY)
    sm = pl.BlockSpec(memory_space=pltpu.SMEM)
    embed, grad_features, g, bias = pl.pallas_call(
        layer_kernel,
        out_shape=(
            jax.ShapeDtypeStruct((1024, 256), BF),
            jax.ShapeDtypeStruct((1024, 256), BF),
            jax.ShapeDtypeStruct((768, 1024), BF),
            jax.ShapeDtypeStruct((16, 128), F32),
        ),
        in_specs=[sm, hbm, hbm, hbm, hbm, vm, hbm, vm, hbm],
        out_specs=(vm, vm, vm, vm),
        scratch_shapes=LAYER_SCRATCH + AR_SCRATCH,
        compiler_params=pltpu.CompilerParams(
            collective_id=0, has_side_effects=True, vmem_limit_bytes=60 << 20
        ),
        name="layer",
    )(
        tile_cols.T, node_features, tile_weights, w_self, w_neigh,
        bias_hidden.reshape(1, 1024), w_out, bias_out.reshape(1, 256), cotangent,
    )
    scale = 1.0 / math.sqrt(1024 * 256)
    g = g.astype(F32) * scale
    bias = bias.reshape(-1) * scale
    return (
        embed, grad_features, g[:256], g[256:512], bias[:1024], g[512:].T, bias[1024:1280],
    )


def solution(mesh):
    in_specs = (
        P(("row", "col"), None),
        P(("row", "col"), None),
        P(("row", "col"), None, None),
        P(),
        P(),
        P(),
        P(),
        P(),
        P(("row", "col"), None),
    )
    out_specs = (P(("row", "col"), None), P(("row", "col"), None), P(), P(), P(), P(), P())
    return jax.shard_map(local, mesh=mesh, in_specs=in_specs, out_specs=out_specs, check_vma=False)
```

```python
import math

import jax
import jax.numpy as jnp
from jax import lax
from jax.experimental import pallas as pl
from jax.experimental.pallas import tpu as pltpu
from jax.sharding import PartitionSpec as P

MESH = pl.DeviceIdType.MESH
BF, F32 = jnp.bfloat16, jnp.float32


def coords():
    row, z_lo = lax.axis_index("row"), lax.axis_index("col")
    core = row % 2
    x = (row // 2) % 4
    y = (row // 8) % 4
    z = (row // 32) * 4 + z_lo
    return row, z_lo, core, x, y, z


def partners():
    row, z_lo, core, x, y, z = coords()
    sibling = [(row + 1 - 2 * core, z_lo, 1 - core)]
    xs = [(row + ((x + d) % 4 - x) * 2, z_lo, (x + d) % 4) for d in (2, 1, 3)]
    ys = [(row + ((y + d) % 4 - y) * 8, z_lo, (y + d) % 4) for d in (2, 1, 3)]
    zs = []
    for d in (4, 3, 5, 2, 6, 1, 7):
        k = (z + d) % 8
        zs.append((row + (k // 4 - z // 4) * 32, k % 4, k))
    return sibling, xs, ys, zs


def remote(src, dst, send, recv, dev):
    return pltpu.make_async_remote_copy(
        src_ref=src, dst_ref=dst, send_sem=send, recv_sem=recv,
        device_id=(dev[0], dev[1]), device_id_type=MESH)


BATCH, HALF, PART = 256, 128, 32


def line_sum(own, line, at):
    total = own
    for dev in line:
        total = total + at(dev[2]).astype(F32)
    return total


def make_reduce(g, bias, gout, bout, rc, s1, r1, t1, r2, zin, rz, zfull, bc, bx, by, bz,
                send, recv):
    row, z_lo, core, x, y, z = coords()
    sibling, xs, ys, zs = partners()
    first = ((xs, x), (ys, y))
    second = ((ys, y), (xs, x))
    sent = []

    def go(src, dst, rsem, dev):
        c = remote(src, dst, send.at[len(sent)], recv.at[rsem], dev)
        c.start()
        sent.append(c)

    def land(dst, rsem):
        remote(dst, dst, send.at[0], recv.at[rsem], sibling[0]).wait_recv()

    mine = pl.ds(pl.multiple_of(core * 512, 512), 512)
    other = pl.ds(pl.multiple_of((1 - core) * 512, 512), 512)

    def batch(b):
        return pl.ds(b * BATCH, BATCH)

    def part(b, h, j):
        return pl.ds(pl.multiple_of(b * BATCH + h * HALF + j * PART, PART), PART)

    def block(j):
        return pl.ds(pl.multiple_of(core * 512 + j * 128, 128), 128)

    def n_core(b):
        return b

    def n_s1(b, h, j):
        return 3 + b * 8 + h * 4 + j

    def n_s2(b, h, j):
        return 27 + b * 8 + h * 4 + j

    def n_z(b, j):
        return 51 + b * 8 + j

    def n_zback(b, j):
        return 75 + b * 8 + j

    def n_s2back(b, h, j):
        return 99 + b * 8 + h * 4 + j

    def n_s1back(b, h, j):
        return 123 + b * 8 + h * 4 + j

    def n_coreback(b, h, j):
        return 147 + b * 8 + h * 4 + j

    n_bias = 171

    def pair(b):
        go(g.at[batch(b), other], rc.at[batch(b), :], n_core(b), sibling[0])

    def pair_bias():
        go(bias, bc, n_bias, sibling[0])

    def over_first(b):
        land(rc.at[batch(b), :], n_core(b))
        for h, (line, me) in enumerate(first):
            s1[pl.ds(b * BATCH + h * HALF, HALF), :] = (
                g[pl.ds(b * BATCH + h * HALF, HALF), mine].astype(F32)
                + rc[pl.ds(b * BATCH + h * HALF, HALF), :].astype(F32)
            ).astype(BF)
        for n in range(3):
            for h, (line, me) in enumerate(first):
                dev = line[n]
                go(s1.at[part(b, h, dev[2]), :], r1.at[b, h, me], n_s1(b, h, me), dev)

    def bias_first():
        land(bc, n_bias)
        bx[x] = bias[...] + bc[...]
        for dev in xs:
            go(bx.at[x], bx.at[x], n_bias + 1 + x, dev)

    def over_second(b):
        for h, (line, me) in enumerate(first):
            for dev in line:
                land(r1.at[b, h, dev[2]], n_s1(b, h, dev[2]))
            total = line_sum(s1[part(b, h, me), :].astype(F32), line, lambda j: r1[b, h, j])
            t1[b, h] = total.astype(BF)
            for dev in second[h][0]:
                lanes = pl.ds(pl.multiple_of(dev[2] * 128, 128), 128)
                m = second[h][1]
                go(t1.at[b, h, :, lanes], r2.at[b, h, m], n_s2(b, h, m), dev)

    def bias_second():
        for dev in xs:
            land(bx.at[dev[2]], n_bias + 1 + dev[2])
        by[y] = bx[0] + bx[1] + bx[2] + bx[3]
        for dev in ys:
            go(by.at[y], by.at[y], n_bias + 5 + y, dev)

    def over_z(b):
        for h, (line, me) in enumerate(second):
            for dev in line:
                land(r2.at[b, h, dev[2]], n_s2(b, h, dev[2]))
            own = t1[b, h, :, pl.ds(pl.multiple_of(me * 128, 128), 128)].astype(F32)
            total = line_sum(own, line, lambda j: r2[b, h, j])
            zin[b, h * 4 : h * 4 + 4] = total.reshape(4, 8, 128)
        for dev in zs:
            go(zin.at[b, dev[2]], rz.at[b, z], n_z(b, z), dev)

    def bias_z():
        for dev in ys:
            land(by.at[dev[2]], n_bias + 5 + dev[2])
        bz[z] = by[0] + by[1] + by[2] + by[3]
        for dev in zs:
            go(bz.at[z], bz.at[z], n_bias + 9 + z, dev)

    def back_z(b):
        for dev in zs:
            land(rz.at[b, dev[2]], n_z(b, dev[2]))
        zfull[b, z] = line_sum(zin[b, z], zs, lambda j: rz[b, j])
        for dev in zs:
            go(zfull.at[b, z], zfull.at[b, z], n_zback(b, z), dev)

    def bias_end():
        for dev in zs:
            land(bz.at[dev[2]], n_bias + 9 + dev[2])
        bout[...] = ((bz[0] + bz[1]) + (bz[2] + bz[3])) + ((bz[4] + bz[5]) + (bz[6] + bz[7]))

    def back_second(b):
        for dev in zs:
            land(zfull.at[b, dev[2]], n_zback(b, dev[2]))
        for h, (line, me) in enumerate(second):
            rows = part(b, h, first[h][1])
            gout[rows, block(me)] = zfull[b, h * 4 : h * 4 + 4].reshape(PART, 128).astype(BF)
            for dev in line:
                go(gout.at[rows, block(me)], gout.at[rows, block(me)], n_s2back(b, h, me), dev)

    def back_first(b):
        for h, (line, me) in enumerate(second):
            own = first[h][1]
            rows = part(b, h, own)
            for dev in line:
                land(gout.at[rows, block(dev[2])], n_s2back(b, h, dev[2]))
            for dev in first[h][0]:
                go(gout.at[rows, mine], gout.at[rows, mine], n_s1back(b, h, own), dev)
            go(gout.at[rows, mine], gout.at[rows, mine], n_coreback(b, h, own), sibling[0])

    def back_pair(b):
        for h, (line, me) in enumerate(first):
            for dev in line:
                rows = part(b, h, dev[2])
                land(gout.at[rows, mine], n_s1back(b, h, dev[2]))
                go(gout.at[rows, mine], gout.at[rows, mine], n_coreback(b, h, dev[2]), sibling[0])

    def back_end(b):
        for h in range(2):
            for j in range(4):
                land(gout.at[part(b, h, j), other], n_coreback(b, h, j))

    def finish():
        for c in sent:
            c.wait_send()

    return dict(pair=pair, pair_bias=pair_bias, over_first=over_first, bias_first=bias_first,
                over_second=over_second, bias_second=bias_second, over_z=over_z, bias_z=bias_z,
                back_z=back_z, bias_end=bias_end, back_second=back_second, back_first=back_first,
                back_pair=back_pair, back_end=back_end, finish=finish)


AR_SCRATCH = [
    pltpu.VMEM((768, 512), BF),
    pltpu.VMEM((768, 512), BF),
    pltpu.VMEM((3, 2, 4, 32, 512), BF),
    pltpu.VMEM((3, 2, 32, 512), BF),
    pltpu.VMEM((3, 2, 4, 32, 128), BF),
    pltpu.VMEM((3, 8, 8, 128), F32),
    pltpu.VMEM((3, 8, 8, 128), F32),
    pltpu.VMEM((3, 8, 8, 128), F32),
    pltpu.VMEM((16, 128), F32),
    pltpu.VMEM((4, 16, 128), F32),
    pltpu.VMEM((4, 16, 128), F32),
    pltpu.VMEM((8, 16, 128), F32),
    pltpu.SemaphoreType.DMA((184,)),
    pltpu.SemaphoreType.DMA((192,)),
]


def greet(devs):
    barrier = pltpu.get_barrier_semaphore()
    for dev in devs:
        pl.semaphore_signal(barrier, inc=1, device_id=(dev[0], dev[1]), device_id_type=MESH)
    pl.semaphore_wait(barrier, len(devs))


SCALE_TILE = 0.25 / math.sqrt(512)
C0 = math.sqrt(2.0 / math.pi)
C1 = C0 * 0.044715
T_RHS = (((1,), (1,)), ((), ()))


def mm(a, b):
    return jnp.dot(a, b, preferred_element_type=F32)


def mm_t(a, b):
    return lax.dot_general(a, b, T_RHS, preferred_element_type=F32)


def ds256(i):
    return pl.ds(pl.multiple_of(i * 256, 256), 256)


SENDS = {0: (0,), 1: (1,), 2: (2,), 3: (7, 3, 6), "back_z": (5, 4)}


def neighbours():
    row, z_lo, core, x, y, z = coords()
    here = row * 4 + z_lo
    right = (here + 1) % 256
    left = (here + 255) % 256
    return here, (left // 4, left % 4), (right // 4, right % 4)


def layer_kernel(
    cols, x_hbm, tw_hbm, ws_hbm, wn_hbm, bh, wo_hbm, bo, cot_hbm,
    embed_hbm, gradf_hbm, gwo_hbm, gws_hbm, gwn_hbm, bout,
    embed, gradf, gout, gwo,
    win, tw, ws, wn, wo, cot, dup, dense, pre, dact, agg0, xt, ct, at,
    hid, dh, da_t, bsum, own, lo, hi, lo_b, hi_b, from_r, from_l, g, bias,
    in_sem, out_sem, halo_send, halo_recv, *ar,
):
    here, left, right = neighbours()
    sibling, xs, ys, zs = partners()

    loads = []
    for n, (src, dst) in enumerate((
        (tw_hbm, tw), (x_hbm, win.at[pl.ds(1024, 1024), :]), (cot_hbm, cot),
        (ws_hbm, ws), (wo_hbm, wo), (wn_hbm, wn),
    )):
        c = pltpu.make_async_copy(src, dst, in_sem.at[n])
        c.start()
        loads.append(c)
    greet([left, right] + sibling + xs + ys + zs)

    halo = []
    writes = []

    def write(src, dst):
        c = pltpu.make_async_copy(src, dst, out_sem.at[len(writes)])
        c.start()
        writes.append(c)

    def halo_copy(src, dst, n, dev):
        c = remote(src, dst, halo_send.at[n], halo_recv.at[n], dev)
        c.start()
        halo.append(c)

    def halo_wait(n):
        dst = win.at[pl.ds(256 * n if n < 4 else 1024 + 256 * n, 256), :]
        remote(dst, dst, halo_send.at[n], halo_recv.at[n], left).wait_recv()

    for i in range(4):
        rows = pl.ds(256 * i, 256)
        halo_copy(x_hbm.at[rows, :], win.at[rows, :], i, right)
    for i in range(4):
        rows = pl.ds(256 * i, 256)
        halo_copy(x_hbm.at[rows, :], win.at[pl.ds(2048 + 256 * i, 256), :], 4 + i, left)

    def build_dense():
        lane = lax.broadcasted_iota(jnp.int32, (64, 128), 1)
        half = lax.broadcasted_iota(jnp.int32, (1, 128), 1) // 64

        @pl.loop(0, 16)
        def _(p):
            c = p // 4
            rows = pl.ds(pl.multiple_of((p % 4) * 64, 64), 64)
            base = here * 16 - 16 + 4 * c
            for q in range(4):
                u = tw[p, :, 128 * q : 128 * q + 128].astype(F32) * SCALE_TILE
                u = u.astype(BF).astype(F32)
                r = pltpu.roll(u, 64, 1)
                dup[2 * q] = jnp.where(lane < 64, u, r)
                dup[2 * q + 1] = jnp.where(lane < 64, r, u)
            spot = [cols[s, p] - base for s in range(8)]

            @pl.loop(0, 18)
            def _(j):
                total = jnp.zeros((64, 128), F32)
                for s in range(8):
                    hit = jnp.where(half == spot[s] - 2 * j, 1.0, 0.0).astype(F32)
                    total = total + dup[s] * hit
                dense[c, rows, pl.ds(pl.multiple_of(j * 128, 128), 128)] = total.astype(BF)

    def local_part():
        bsum[...] = jnp.zeros_like(bsum)

        @pl.loop(0, 4)
        def _(c):
            rows = ds256(c)
            mine = pl.ds(pl.multiple_of(1024 + c * 256, 256), 256)
            xc = win[mine, :]
            cc = cot[rows, :]
            xt[:, rows] = xc.T
            ct[:, rows] = cc.T
            bsum[:, 1024:1280] += jnp.sum(cc.astype(F32).reshape(32, 8, 256), axis=0)
            for n in range(4):
                n4 = slice(256 * n, 256 * n + 256)
                pre[rows, n4] = mm(xc, ws[:, n4]) + bh[:, n4]
                dact[rows, n4] = mm_t(cc, wo[n4, :])
            total = jnp.zeros((256, 256), F32)
            for t in range(4):
                total = total + mm(dense[c, :, ds256(4 + t - c)], win[1024 + 256 * t : 1280 + 256 * t, :])
            agg0[rows, :] = total

    def low_part():
        for c in range(4):
            rows = slice(256 * c, 256 * c + 256)
            total = agg0[rows, :]
            for t in range(c, 4):
                total = total + mm(dense[c, :, 256 * (t - c) : 256 * (t - c) + 256], win[256 * t : 256 * t + 256, :])
            agg0[rows, :] = total

    def adjoint_round(n):
        j = n % 4
        src, buf = ((lo, lo_b), (hi, hi_b))[n // 4]
        buf[j] = src[:, 256 * j : 256 * j + 256].astype(BF)

    def adjoint_send(pieces):
        for n in pieces:
            j = n % 4
            buf, dst, dev = ((lo_b, from_r, left), (hi_b, from_l, right))[n // 4]
            halo_copy(buf.at[j], dst.at[j], 8 + n, dev)

    def chunk(c):
        r4 = slice(256 * c, 256 * c + 256)
        total = agg0[r4, :]
        for t in range(c + 1):
            b = 256 * (8 + t - c)
            total = total + mm(dense[c, :, b : b + 256], win[2048 + 256 * t : 2304 + 256 * t, :])
        ag = total.astype(BF)
        for n in range(4):
            n4 = slice(256 * n, 256 * n + 256)
            pre[r4, n4] += mm(ag, wn[:, n4])
        at[:, r4] = ag.T

        @pl.loop(0, 8)
        def _(i):
            r = pl.ds(pl.multiple_of(c * 256 + i * 32, 32), 32)
            for n in range(4):
                n4 = slice(256 * n, 256 * n + 256)
                v = pre[r, n4]
                u = v * v
                a = 0.5 * jnp.tanh(v * (C0 + C1 * u)) + 0.5
                h = v * a
                hid[r, n4] = h.astype(BF)
                slope = a + h * ((2.0 * C0) + (6.0 * C1) * u) * (1.0 - a)
                d = (dact[r, n4] * slope).astype(BF)
                dh[r, n4] = d
                bsum[:, n4] += jnp.sum(d.astype(F32).reshape(4, 8, 256), axis=0)

        da = mm_t(wn[...], dh[r4, :]).astype(BF)
        da_t[c] = da
        for j in range(c, 4):
            part = mm(da, dense[c, :, 256 * (j - c) : 256 * (j - c) + 256])
            j4 = slice(256 * j, 256 * j + 256)
            lo[:, j4] = part if c == 0 else lo[:, j4] + part
            if j == c:
                adjoint_round(j)
        for j in range(c + 1):
            b = 256 * (8 + j - c)
            part = mm(da, dense[c, :, b : b + 256])
            j4 = slice(256 * j, 256 * j + 256)
            hi[:, j4] = part if c == j else hi[:, j4] + part
            if c == 3:
                adjoint_round(4 + j)

    def weight_grad(b):
        left_side, right_side = ((ct, hid), (xt, dh), (at, dh))[b]
        for n in range(4):
            n4 = slice(256 * n, 256 * n + 256)
            g[256 * b : 256 * b + 256, n4] = mm(left_side[...], right_side[:, n4]).astype(BF)

    def bias_grads():
        sums = jnp.sum(bsum[...], axis=0, keepdims=True)
        for n in range(10):
            bias[n : n + 1, :] = sums[:, 128 * n : 128 * n + 128]
        bias[10:16, :] = jnp.zeros((6, 128), F32)

    def local_rest():
        @pl.loop(0, 4)
        def _(c):
            rows = ds256(c)
            embed[rows, :] = (mm(hid[rows, :], wo[...]) + bo[...]).astype(BF)
            total = jnp.zeros((256, 256), F32)
            for b in range(4):
                total = total + mm(da_t[b], dense[b, :, ds256(4 + c - b)])
            own[rows, :] = mm_t(dh[rows, :], ws[...]) + total.T

    def last_sum():
        for j in (0, 1, 2, 3):
            for m, dst in ((j, from_r), (4 + j, from_l)):
                remote(dst.at[j], dst.at[j], halo_send.at[8 + m], halo_recv.at[8 + m], left).wait_recv()
            rows = slice(256 * j, 256 * j + 256)
            outer = from_l[j].astype(F32) + from_r[j].astype(F32)
            gradf[rows, :] = (own[rows, :] + outer.T).astype(BF)

    loads[0].wait()
    build_dense()
    for c in loads[1:]:
        c.wait()
    local_part()
    for n in range(4):
        halo_wait(n)
    low_part()
    for c in range(4):
        halo_wait(4 + c)
        chunk(c)
        adjoint_send(SENDS[c])
    red = make_reduce(g, bias, gout, bout, *ar)
    weight_grad(0)
    red["pair"](0)
    weight_grad(1)
    red["pair"](1)
    red["over_first"](0)
    weight_grad(2)
    red["pair"](2)
    bias_grads()
    red["pair_bias"]()
    red["over_first"](1)
    red["over_first"](2)
    red["bias_first"]()
    local_rest()
    write(embed, embed_hbm)
    for stage in ("over_second", "over_z", "back_z", "back_second", "back_first"):
        for b in range(3):
            red[stage](b)
        adjoint_send(SENDS.get(stage, ()))
        tail = {"over_second": "bias_second", "over_z": "bias_z", "back_z": "bias_end"}.get(stage)
        if tail is not None:
            red[tail]()
    last_sum()
    write(gradf, gradf_hbm)
    for b in range(3):
        red["back_pair"](b)
    red["back_end"](0)
    for n in range(4):
        n4 = slice(256 * n, 256 * n + 256)
        gwo[n4, :] = gout[0:256, n4].T
    write(gwo, gwo_hbm)
    red["back_end"](1)
    write(gout.at[pl.ds(256, 256), :], gws_hbm)
    red["back_end"](2)
    write(gout.at[pl.ds(512, 256), :], gwn_hbm)
    red["finish"]()
    for c in halo:
        c.wait_send()
    for c in writes:
        c.wait()


LAYER_SCRATCH = [
    pltpu.VMEM((1024, 256), BF),
    pltpu.VMEM((1024, 256), BF),
    pltpu.VMEM((768, 1024), BF),
    pltpu.VMEM((1024, 256), BF),
    pltpu.VMEM((3072, 256), BF),
    pltpu.VMEM((16, 64, 512), jnp.int32),
    pltpu.VMEM((256, 1024), BF),
    pltpu.VMEM((256, 1024), BF),
    pltpu.VMEM((1024, 256), BF),
    pltpu.VMEM((1024, 256), BF),
    pltpu.VMEM((8, 64, 128), F32),
    pltpu.VMEM((4, 256, 2304), BF),
    pltpu.VMEM((1024, 1024), F32),
    pltpu.VMEM((1024, 1024), F32),
    pltpu.VMEM((1024, 256), F32),
    pltpu.VMEM((256, 1024), BF),
    pltpu.VMEM((256, 1024), BF),
    pltpu.VMEM((256, 1024), BF),
    pltpu.VMEM((1024, 1024), BF),
    pltpu.VMEM((1024, 1024), BF),
    pltpu.VMEM((4, 256, 256), BF),
    pltpu.VMEM((8, 1280), F32),
    pltpu.VMEM((1024, 256), F32),
    pltpu.VMEM((256, 1024), F32),
    pltpu.VMEM((256, 1024), F32),
    pltpu.VMEM((4, 256, 256), BF),
    pltpu.VMEM((4, 256, 256), BF),
    pltpu.VMEM((4, 256, 256), BF),
    pltpu.VMEM((4, 256, 256), BF),
    pltpu.VMEM((768, 1024), BF),
    pltpu.VMEM((16, 128), F32),
    pltpu.SemaphoreType.DMA((6,)),
    pltpu.SemaphoreType.DMA((5,)),
    pltpu.SemaphoreType.DMA((16,)),
    pltpu.SemaphoreType.DMA((16,)),
]


def local(
    node_features, tile_cols, tile_weights, w_self, w_neigh, bias_hidden, w_out, bias_out, cotangent
):
    vm = pl.BlockSpec(memory_space=pltpu.VMEM)
    hbm = pl.BlockSpec(memory_space=pl.ANY)
    sm = pl.BlockSpec(memory_space=pltpu.SMEM)
    embed, grad_features, gwo, gws, gwn, bias = pl.pallas_call(
        layer_kernel,
        out_shape=(
            jax.ShapeDtypeStruct((1024, 256), BF),
            jax.ShapeDtypeStruct((1024, 256), BF),
            jax.ShapeDtypeStruct((1024, 256), BF),
            jax.ShapeDtypeStruct((256, 1024), BF),
            jax.ShapeDtypeStruct((256, 1024), BF),
            jax.ShapeDtypeStruct((16, 128), F32),
        ),
        in_specs=[sm, hbm, hbm, hbm, hbm, vm, hbm, vm, hbm],
        out_specs=(hbm, hbm, hbm, hbm, hbm, vm),
        scratch_shapes=LAYER_SCRATCH + AR_SCRATCH,
        compiler_params=pltpu.CompilerParams(
            collective_id=0, has_side_effects=True, vmem_limit_bytes=60 << 20
        ),
        name="layer",
    )(
        tile_cols.T, node_features, tile_weights, w_self, w_neigh,
        bias_hidden.reshape(1, 1024), w_out, bias_out.reshape(1, 256), cotangent,
    )
    scale = 1.0 / math.sqrt(1024 * 256)
    bias = bias.reshape(-1) * scale
    return (
        embed,
        grad_features,
        gws.astype(F32) * scale,
        gwn.astype(F32) * scale,
        bias[:1024],
        gwo.astype(F32) * scale,
        bias[1024:1280],
    )


def solution(mesh):
    in_specs = (
        P(("row", "col"), None),
        P(("row", "col"), None),
        P(("row", "col"), None, None),
        P(),
        P(),
        P(),
        P(),
        P(),
        P(("row", "col"), None),
    )
    out_specs = (P(("row", "col"), None), P(("row", "col"), None), P(), P(), P(), P(), P())
    return jax.shard_map(local, mesh=mesh, in_specs=in_specs, out_specs=out_specs, check_vma=False)
```

```python
import math

import jax
import jax.numpy as jnp
from jax import lax
from jax.experimental import pallas as pl
from jax.experimental.pallas import tpu as pltpu
from jax.sharding import PartitionSpec as P

MESH = pl.DeviceIdType.MESH
BF, F32 = jnp.bfloat16, jnp.float32


def coords():
    row, z_lo = lax.axis_index("row"), lax.axis_index("col")
    core = row % 2
    x = (row // 2) % 4
    y = (row // 8) % 4
    z = (row // 32) * 4 + z_lo
    return row, z_lo, core, x, y, z


def partners():
    row, z_lo, core, x, y, z = coords()
    sibling = [(row + 1 - 2 * core, z_lo, 1 - core)]
    xs = [(row + ((x + d) % 4 - x) * 2, z_lo, (x + d) % 4) for d in (2, 1, 3)]
    ys = [(row + ((y + d) % 4 - y) * 8, z_lo, (y + d) % 4) for d in (2, 1, 3)]
    zs = []
    for d in (4, 3, 5, 2, 6, 1, 7):
        k = (z + d) % 8
        zs.append((row + (k // 4 - z // 4) * 32, k % 4, k))
    return sibling, xs, ys, zs


def remote(src, dst, send, recv, dev):
    return pltpu.make_async_remote_copy(
        src_ref=src, dst_ref=dst, send_sem=send, recv_sem=recv,
        device_id=(dev[0], dev[1]), device_id_type=MESH)


BATCH, HALF, PART = 256, 128, 32


def line_sum(own, line, at):
    total = own
    for dev in line:
        total = total + at(dev[2]).astype(F32)
    return total


def make_reduce(g, bias, gout, bout, rc, s1, r1, t1, r2, zin, rz, zfull, bc, bx, by, bz,
                send, recv):
    row, z_lo, core, x, y, z = coords()
    sibling, xs, ys, zs = partners()
    first = ((xs, x), (ys, y))
    second = ((ys, y), (xs, x))
    sent = []

    def go(src, dst, rsem, dev):
        c = remote(src, dst, send.at[len(sent)], recv.at[rsem], dev)
        c.start()
        sent.append(c)

    def land(dst, rsem):
        remote(dst, dst, send.at[0], recv.at[rsem], sibling[0]).wait_recv()

    mine = pl.ds(pl.multiple_of(core * 512, 512), 512)
    other = pl.ds(pl.multiple_of((1 - core) * 512, 512), 512)

    def batch(b):
        return pl.ds(b * BATCH, BATCH)

    def part(b, h, j):
        return pl.ds(pl.multiple_of(b * BATCH + h * HALF + j * PART, PART), PART)

    def block(j):
        return pl.ds(pl.multiple_of(core * 512 + j * 128, 128), 128)

    def n_core(b):
        return b

    def n_s1(b, h, j):
        return 3 + b * 8 + h * 4 + j

    def n_s2(b, h, j):
        return 27 + b * 8 + h * 4 + j

    def n_z(b, j):
        return 51 + b * 8 + j

    def n_zback(b, j):
        return 75 + b * 8 + j

    def n_s2back(b, h, j):
        return 99 + b * 8 + h * 4 + j

    def n_s1back(b, h, j):
        return 123 + b * 8 + h * 4 + j

    def n_coreback(b, h, j):
        return 147 + b * 8 + h * 4 + j

    n_bias = 171

    def pair(b):
        go(g.at[batch(b), other], rc.at[batch(b), :], n_core(b), sibling[0])

    def pair_bias():
        go(bias, bc, n_bias, sibling[0])

    def over_first(b):
        land(rc.at[batch(b), :], n_core(b))
        for h, (line, me) in enumerate(first):
            s1[pl.ds(b * BATCH + h * HALF, HALF), :] = (
                g[pl.ds(b * BATCH + h * HALF, HALF), mine].astype(F32)
                + rc[pl.ds(b * BATCH + h * HALF, HALF), :].astype(F32)
            ).astype(BF)
        for n in range(3):
            for h, (line, me) in enumerate(first):
                dev = line[n]
                go(s1.at[part(b, h, dev[2]), :], r1.at[b, h, me], n_s1(b, h, me), dev)

    def bias_first():
        land(bc, n_bias)
        bx[x] = bias[...] + bc[...]
        for dev in xs:
            go(bx.at[x], bx.at[x], n_bias + 1 + x, dev)

    def over_second(b):
        for h, (line, me) in enumerate(first):
            for dev in line:
                land(r1.at[b, h, dev[2]], n_s1(b, h, dev[2]))
            total = line_sum(s1[part(b, h, me), :].astype(F32), line, lambda j: r1[b, h, j])
            t1[b, h] = total.astype(BF)
            for dev in second[h][0]:
                lanes = pl.ds(pl.multiple_of(dev[2] * 128, 128), 128)
                m = second[h][1]
                go(t1.at[b, h, :, lanes], r2.at[b, h, m], n_s2(b, h, m), dev)

    def bias_second():
        for dev in xs:
            land(bx.at[dev[2]], n_bias + 1 + dev[2])
        by[y] = bx[0] + bx[1] + bx[2] + bx[3]
        for dev in ys:
            go(by.at[y], by.at[y], n_bias + 5 + y, dev)

    def over_z(b):
        for h, (line, me) in enumerate(second):
            for dev in line:
                land(r2.at[b, h, dev[2]], n_s2(b, h, dev[2]))
            own = t1[b, h, :, pl.ds(pl.multiple_of(me * 128, 128), 128)].astype(F32)
            total = line_sum(own, line, lambda j: r2[b, h, j])
            zin[b, h * 4 : h * 4 + 4] = total.reshape(4, 8, 128)
        for dev in zs:
            go(zin.at[b, dev[2]], rz.at[b, z], n_z(b, z), dev)

    def bias_z():
        for dev in ys:
            land(by.at[dev[2]], n_bias + 5 + dev[2])
        bz[z] = by[0] + by[1] + by[2] + by[3]
        for dev in zs:
            go(bz.at[z], bz.at[z], n_bias + 9 + z, dev)

    def back_z(b):
        for dev in zs:
            land(rz.at[b, dev[2]], n_z(b, dev[2]))
        zfull[b, z] = line_sum(zin[b, z], zs, lambda j: rz[b, j])
        for dev in zs:
            go(zfull.at[b, z], zfull.at[b, z], n_zback(b, z), dev)

    def bias_end():
        for dev in zs:
            land(bz.at[dev[2]], n_bias + 9 + dev[2])
        bout[...] = ((bz[0] + bz[1]) + (bz[2] + bz[3])) + ((bz[4] + bz[5]) + (bz[6] + bz[7]))

    def back_second(b):
        for dev in zs:
            land(zfull.at[b, dev[2]], n_zback(b, dev[2]))
        for h, (line, me) in enumerate(second):
            rows = part(b, h, first[h][1])
            gout[rows, block(me)] = zfull[b, h * 4 : h * 4 + 4].reshape(PART, 128).astype(BF)
            for dev in line:
                go(gout.at[rows, block(me)], gout.at[rows, block(me)], n_s2back(b, h, me), dev)

    def back_first(b):
        for h, (line, me) in enumerate(second):
            own = first[h][1]
            rows = part(b, h, own)
            for dev in line:
                land(gout.at[rows, block(dev[2])], n_s2back(b, h, dev[2]))
            for dev in first[h][0]:
                go(gout.at[rows, mine], gout.at[rows, mine], n_s1back(b, h, own), dev)
            go(gout.at[rows, mine], gout.at[rows, mine], n_coreback(b, h, own), sibling[0])

    def back_pair(b):
        for h, (line, me) in enumerate(first):
            for dev in line:
                rows = part(b, h, dev[2])
                land(gout.at[rows, mine], n_s1back(b, h, dev[2]))
                go(gout.at[rows, mine], gout.at[rows, mine], n_coreback(b, h, dev[2]), sibling[0])

    def back_end(b):
        for h in range(2):
            for j in range(4):
                land(gout.at[part(b, h, j), other], n_coreback(b, h, j))

    def finish():
        for c in sent:
            c.wait_send()

    return dict(pair=pair, pair_bias=pair_bias, over_first=over_first, bias_first=bias_first,
                over_second=over_second, bias_second=bias_second, over_z=over_z, bias_z=bias_z,
                back_z=back_z, bias_end=bias_end, back_second=back_second, back_first=back_first,
                back_pair=back_pair, back_end=back_end, finish=finish)


AR_SCRATCH = [
    pltpu.VMEM((768, 512), BF),
    pltpu.VMEM((768, 512), BF),
    pltpu.VMEM((3, 2, 4, 32, 512), BF),
    pltpu.VMEM((3, 2, 32, 512), BF),
    pltpu.VMEM((3, 2, 4, 32, 128), BF),
    pltpu.VMEM((3, 8, 8, 128), F32),
    pltpu.VMEM((3, 8, 8, 128), F32),
    pltpu.VMEM((3, 8, 8, 128), F32),
    pltpu.VMEM((16, 128), F32),
    pltpu.VMEM((4, 16, 128), F32),
    pltpu.VMEM((4, 16, 128), F32),
    pltpu.VMEM((8, 16, 128), F32),
    pltpu.SemaphoreType.DMA((184,)),
    pltpu.SemaphoreType.DMA((192,)),
]


def greet(devs):
    barrier = pltpu.get_barrier_semaphore()
    for dev in devs:
        pl.semaphore_signal(barrier, inc=1, device_id=(dev[0], dev[1]), device_id_type=MESH)
    pl.semaphore_wait(barrier, len(devs))


SCALE_TILE = 0.25 / math.sqrt(512)
C0 = math.sqrt(2.0 / math.pi)
C1 = C0 * 0.044715
T_RHS = (((1,), (1,)), ((), ()))


def mm(a, b):
    return jnp.dot(a, b, preferred_element_type=F32)


def mm_t(a, b):
    return lax.dot_general(a, b, T_RHS, preferred_element_type=F32)


def ds256(i):
    return pl.ds(pl.multiple_of(i * 256, 256), 256)


SENDS = {0: (0,), 1: (1,), 2: (2,), 3: (7, 3, 6), "back_z": (5, 4)}


def neighbours():
    row, z_lo, core, x, y, z = coords()
    here = row * 4 + z_lo
    right = (here + 1) % 256
    left = (here + 255) % 256
    return here, (left // 4, left % 4), (right // 4, right % 4)


def layer_kernel(
    cols, x_hbm, tw_hbm, ws_hbm, wn_hbm, bh, wo_hbm, bo, cot_hbm,
    embed_hbm, gradf_hbm, gwo_hbm, gws_hbm, gwn_hbm, bout,
    embed, gradf, gout, gwo,
    win, tw, ws, wn, wo, cot, dup, dense, pre, dact, agg0, xt, ct, at,
    hid, dh, da_t, bsum, own, lo, hi, lo_b, hi_b, from_r, from_l, g, bias,
    in_sem, out_sem, halo_send, halo_recv, *ar,
):
    here, left, right = neighbours()
    sibling, xs, ys, zs = partners()

    loads = []
    for n, (src, dst) in enumerate((
        (tw_hbm, tw), (x_hbm, win.at[pl.ds(1024, 1024), :]), (cot_hbm, cot),
        (ws_hbm, ws), (wo_hbm, wo), (wn_hbm, wn),
    )):
        c = pltpu.make_async_copy(src, dst, in_sem.at[n])
        c.start()
        loads.append(c)
    greet([left, right] + sibling + xs + ys + zs)

    halo = []
    writes = []

    def write(src, dst):
        c = pltpu.make_async_copy(src, dst, out_sem.at[len(writes)])
        c.start()
        writes.append(c)

    def halo_copy(src, dst, n, dev):
        c = remote(src, dst, halo_send.at[n], halo_recv.at[n], dev)
        c.start()
        halo.append(c)

    def halo_wait(n):
        dst = win.at[pl.ds(256 * n if n < 4 else 1024 + 256 * n, 256), :]
        remote(dst, dst, halo_send.at[n], halo_recv.at[n], left).wait_recv()

    for i in range(4):
        rows = pl.ds(256 * i, 256)
        halo_copy(x_hbm.at[rows, :], win.at[rows, :], i, right)
    for i in range(4):
        rows = pl.ds(256 * i, 256)
        halo_copy(x_hbm.at[rows, :], win.at[pl.ds(2048 + 256 * i, 256), :], 4 + i, left)

    def build_dense():
        lane = lax.broadcasted_iota(jnp.int32, (64, 128), 1)
        half = lax.broadcasted_iota(jnp.int32, (1, 128), 1) // 64

        @pl.loop(0, 16)
        def _(p):
            c = p // 4
            rows = pl.ds(pl.multiple_of((p % 4) * 64, 64), 64)
            base = here * 16 - 16 + 4 * c
            for q in range(4):
                u = tw[p, :, 128 * q : 128 * q + 128].astype(F32) * SCALE_TILE
                u = u.astype(BF).astype(F32)
                r = pltpu.roll(u, 64, 1)
                dup[2 * q] = jnp.where(lane < 64, u, r)
                dup[2 * q + 1] = jnp.where(lane < 64, r, u)
            spot = [cols[s, p] - base for s in range(8)]

            @pl.loop(0, 18)
            def _(j):
                total = jnp.zeros((64, 128), F32)
                for s in range(8):
                    hit = jnp.where(half == spot[s] - 2 * j, 1.0, 0.0).astype(F32)
                    total = total + dup[s] * hit
                dense[c, rows, pl.ds(pl.multiple_of(j * 128, 128), 128)] = total.astype(BF)

    def local_part():
        bsum[...] = jnp.zeros_like(bsum)

        @pl.loop(0, 4)
        def _(c):
            rows = ds256(c)
            mine = pl.ds(pl.multiple_of(1024 + c * 256, 256), 256)
            xc = win[mine, :]
            cc = cot[rows, :]
            xt[:, rows] = xc.T
            ct[:, rows] = cc.T
            bsum[:, 1024:1280] += jnp.sum(cc.astype(F32).reshape(32, 8, 256), axis=0)
            for n in range(4):
                n4 = slice(256 * n, 256 * n + 256)
                pre[rows, n4] = mm(xc, ws[:, n4]) + bh[:, n4]
                dact[rows, n4] = mm_t(cc, wo[n4, :])
            total = jnp.zeros((256, 256), F32)
            for t in range(4):
                total = total + mm(dense[c, :, ds256(4 + t - c)], win[1024 + 256 * t : 1280 + 256 * t, :])
            agg0[rows, :] = total

    def low_part():
        for c in range(4):
            rows = slice(256 * c, 256 * c + 256)
            total = agg0[rows, :]
            for t in range(c, 4):
                total = total + mm(dense[c, :, 256 * (t - c) : 256 * (t - c) + 256], win[256 * t : 256 * t + 256, :])
            agg0[rows, :] = total

    def adjoint_round(n):
        j = n % 4
        src, buf = ((lo, lo_b), (hi, hi_b))[n // 4]
        buf[j] = src[:, 256 * j : 256 * j + 256].astype(BF)

    def adjoint_send(pieces):
        for n in pieces:
            j = n % 4
            buf, dst, dev = ((lo_b, from_r, left), (hi_b, from_l, right))[n // 4]
            halo_copy(buf.at[j], dst.at[j], 8 + n, dev)

    def chunk(c):
        r4 = slice(256 * c, 256 * c + 256)
        total = agg0[r4, :]
        for t in range(c + 1):
            b = 256 * (8 + t - c)
            total = total + mm(dense[c, :, b : b + 256], win[2048 + 256 * t : 2304 + 256 * t, :])
        ag = total.astype(BF)
        for n in range(4):
            n4 = slice(256 * n, 256 * n + 256)
            pre[r4, n4] += mm(ag, wn[:, n4])
        at[:, r4] = ag.T

        @pl.loop(0, 8)
        def _(i):
            r = pl.ds(pl.multiple_of(c * 256 + i * 32, 32), 32)
            for n in range(4):
                n4 = slice(256 * n, 256 * n + 256)
                v = pre[r, n4]
                u = v * v
                a = 0.5 * jnp.tanh(v * (C0 + C1 * u)) + 0.5
                h = v * a
                hid[r, n4] = h.astype(BF)
                slope = a + h * ((2.0 * C0) + (6.0 * C1) * u) * (1.0 - a)
                d = (dact[r, n4] * slope).astype(BF)
                dh[r, n4] = d
                bsum[:, n4] += jnp.sum(d.astype(F32).reshape(4, 8, 256), axis=0)

    def adjoint(c):
        r4 = slice(256 * c, 256 * c + 256)
        da = mm_t(wn[...], dh[r4, :]).astype(BF)
        da_t[c] = da
        for j in range(c, 4):
            part = mm(da, dense[c, :, 256 * (j - c) : 256 * (j - c) + 256])
            j4 = slice(256 * j, 256 * j + 256)
            lo[:, j4] = part if c == 0 else lo[:, j4] + part
            if j == c:
                adjoint_round(j)
        for j in range(c + 1):
            b = 256 * (8 + j - c)
            part = mm(da, dense[c, :, b : b + 256])
            j4 = slice(256 * j, 256 * j + 256)
            hi[:, j4] = part if c == j else hi[:, j4] + part
            if c == 3:
                adjoint_round(4 + j)

    def weight_grad(b):
        left_side, right_side = ((ct, hid), (xt, dh), (at, dh))[b]
        for n in range(4):
            n4 = slice(256 * n, 256 * n + 256)
            g[256 * b : 256 * b + 256, n4] = mm(left_side[...], right_side[:, n4]).astype(BF)

    def bias_grads():
        sums = jnp.sum(bsum[...], axis=0, keepdims=True)
        for n in range(10):
            bias[n : n + 1, :] = sums[:, 128 * n : 128 * n + 128]
        bias[10:16, :] = jnp.zeros((6, 128), F32)

    def local_rest():
        @pl.loop(0, 4)
        def _(c):
            rows = ds256(c)
            embed[rows, :] = (mm(hid[rows, :], wo[...]) + bo[...]).astype(BF)
            total = jnp.zeros((256, 256), F32)
            for b in range(4):
                total = total + mm(da_t[b], dense[b, :, ds256(4 + c - b)])
            own[rows, :] = mm_t(dh[rows, :], ws[...]) + total.T

    def last_sum():
        for j in (0, 1, 2, 3):
            for m, dst in ((j, from_r), (4 + j, from_l)):
                remote(dst.at[j], dst.at[j], halo_send.at[8 + m], halo_recv.at[8 + m], left).wait_recv()
            rows = slice(256 * j, 256 * j + 256)
            outer = from_l[j].astype(F32) + from_r[j].astype(F32)
            gradf[rows, :] = (own[rows, :] + outer.T).astype(BF)

    loads[0].wait()
    build_dense()
    for c in loads[1:]:
        c.wait()
    local_part()
    for n in range(4):
        halo_wait(n)
    low_part()
    red = make_reduce(g, bias, gout, bout, *ar)
    for c in range(4):
        halo_wait(4 + c)
        chunk(c)
        if c == 3:
            weight_grad(0)
            red["pair"](0)
        adjoint(c)
        adjoint_send(SENDS[c])
    red["over_first"](0)
    weight_grad(1)
    red["pair"](1)
    weight_grad(2)
    red["pair"](2)
    red["over_first"](1)
    bias_grads()
    red["pair_bias"]()
    red["over_first"](2)
    red["bias_first"]()
    local_rest()
    write(embed, embed_hbm)
    for stage in ("over_second", "over_z", "back_z", "back_second", "back_first"):
        for b in range(3):
            red[stage](b)
        adjoint_send(SENDS.get(stage, ()))
        tail = {"over_second": "bias_second", "over_z": "bias_z", "back_z": "bias_end"}.get(stage)
        if tail is not None:
            red[tail]()
    last_sum()
    write(gradf, gradf_hbm)
    for b in range(3):
        red["back_pair"](b)
    red["back_end"](0)
    for n in range(4):
        n4 = slice(256 * n, 256 * n + 256)
        gwo[n4, :] = gout[0:256, n4].T
    write(gwo, gwo_hbm)
    red["back_end"](1)
    write(gout.at[pl.ds(256, 256), :], gws_hbm)
    red["back_end"](2)
    write(gout.at[pl.ds(512, 256), :], gwn_hbm)
    red["finish"]()
    for c in halo:
        c.wait_send()
    for c in writes:
        c.wait()


LAYER_SCRATCH = [
    pltpu.VMEM((1024, 256), BF),
    pltpu.VMEM((1024, 256), BF),
    pltpu.VMEM((768, 1024), BF),
    pltpu.VMEM((1024, 256), BF),
    pltpu.VMEM((3072, 256), BF),
    pltpu.VMEM((16, 64, 512), jnp.int32),
    pltpu.VMEM((256, 1024), BF),
    pltpu.VMEM((256, 1024), BF),
    pltpu.VMEM((1024, 256), BF),
    pltpu.VMEM((1024, 256), BF),
    pltpu.VMEM((8, 64, 128), F32),
    pltpu.VMEM((4, 256, 2304), BF),
    pltpu.VMEM((1024, 1024), F32),
    pltpu.VMEM((1024, 1024), F32),
    pltpu.VMEM((1024, 256), F32),
    pltpu.VMEM((256, 1024), BF),
    pltpu.VMEM((256, 1024), BF),
    pltpu.VMEM((256, 1024), BF),
    pltpu.VMEM((1024, 1024), BF),
    pltpu.VMEM((1024, 1024), BF),
    pltpu.VMEM((4, 256, 256), BF),
    pltpu.VMEM((8, 1280), F32),
    pltpu.VMEM((1024, 256), F32),
    pltpu.VMEM((256, 1024), F32),
    pltpu.VMEM((256, 1024), F32),
    pltpu.VMEM((4, 256, 256), BF),
    pltpu.VMEM((4, 256, 256), BF),
    pltpu.VMEM((4, 256, 256), BF),
    pltpu.VMEM((4, 256, 256), BF),
    pltpu.VMEM((768, 1024), BF),
    pltpu.VMEM((16, 128), F32),
    pltpu.SemaphoreType.DMA((6,)),
    pltpu.SemaphoreType.DMA((5,)),
    pltpu.SemaphoreType.DMA((16,)),
    pltpu.SemaphoreType.DMA((16,)),
]


def scale_kernel(embed, gradf, gws, gwn, bias, gwo, embed_o, gradf_o, gws_o, gwn_o, bh_o, gwo_o, bo_o):
    scale = 1.0 / math.sqrt(1024 * 256)
    embed_o[...] = embed[...]
    gradf_o[...] = gradf[...]
    gws_o[...] = gws[...].astype(F32) * scale
    gwn_o[...] = gwn[...].astype(F32) * scale
    gwo_o[...] = gwo[...].astype(F32) * scale
    bh_o[...] = bias[0:8, :] * scale
    bo_o[...] = bias[8:10, :] * scale


def scaled_outputs(embed, gradf, gws, gwn, bias, gwo):
    steps = 4
    tall = pl.BlockSpec((1024 // steps, 256), lambda i: (i, 0))
    wide = pl.BlockSpec((256 // steps, 1024), lambda i: (i, 0))

    def whole(rows):
        return pl.BlockSpec((rows, 128), lambda i: (0, 0))

    embed, gradf, gws, gwn, bh, gwo, bo = pl.pallas_call(
        scale_kernel,
        grid=(steps,),
        out_shape=(
            jax.ShapeDtypeStruct((1024, 256), BF),
            jax.ShapeDtypeStruct((1024, 256), BF),
            jax.ShapeDtypeStruct((256, 1024), F32),
            jax.ShapeDtypeStruct((256, 1024), F32),
            jax.ShapeDtypeStruct((8, 128), F32),
            jax.ShapeDtypeStruct((1024, 256), F32),
            jax.ShapeDtypeStruct((2, 128), F32),
        ),
        in_specs=[tall, tall, wide, wide, whole(16), tall],
        out_specs=(tall, tall, wide, wide, whole(8), tall, whole(2)),
        name="scaled_outputs",
    )(embed, gradf, gws, gwn, bias, gwo)
    return embed, gradf, gws, gwn, bh.reshape(1024), gwo, bo.reshape(256)


def local(
    node_features, tile_cols, tile_weights, w_self, w_neigh, bias_hidden, w_out, bias_out, cotangent
):
    vm = pl.BlockSpec(memory_space=pltpu.VMEM)
    hbm = pl.BlockSpec(memory_space=pl.ANY)
    sm = pl.BlockSpec(memory_space=pltpu.SMEM)
    embed, grad_features, gwo, gws, gwn, bias = pl.pallas_call(
        layer_kernel,
        out_shape=(
            jax.ShapeDtypeStruct((1024, 256), BF),
            jax.ShapeDtypeStruct((1024, 256), BF),
            jax.ShapeDtypeStruct((1024, 256), BF),
            jax.ShapeDtypeStruct((256, 1024), BF),
            jax.ShapeDtypeStruct((256, 1024), BF),
            jax.ShapeDtypeStruct((16, 128), F32),
        ),
        in_specs=[sm, hbm, hbm, hbm, hbm, vm, hbm, vm, hbm],
        out_specs=(hbm, hbm, hbm, hbm, hbm, vm),
        scratch_shapes=LAYER_SCRATCH + AR_SCRATCH,
        compiler_params=pltpu.CompilerParams(
            collective_id=0, has_side_effects=True, vmem_limit_bytes=60 << 20
        ),
        name="layer",
    )(
        tile_cols.T, node_features, tile_weights, w_self, w_neigh,
        bias_hidden.reshape(1, 1024), w_out, bias_out.reshape(1, 256), cotangent,
    )
    return scaled_outputs(embed, grad_features, gws, gwn, bias, gwo)


def solution(mesh):
    in_specs = (
        P(("row", "col"), None),
        P(("row", "col"), None),
        P(("row", "col"), None, None),
        P(),
        P(),
        P(),
        P(),
        P(),
        P(("row", "col"), None),
    )
    out_specs = (P(("row", "col"), None), P(("row", "col"), None), P(), P(), P(), P(), P())
    return jax.shard_map(local, mesh=mesh, in_specs=in_specs, out_specs=out_specs, check_vma=False)
```

```python
import math

import jax
import jax.numpy as jnp
from jax import lax
from jax.experimental import pallas as pl
from jax.experimental.pallas import tpu as pltpu
from jax.sharding import PartitionSpec as P

MESH = pl.DeviceIdType.MESH
BF, F32 = jnp.bfloat16, jnp.float32


def coords():
    row, z_lo = lax.axis_index("row"), lax.axis_index("col")
    core = row % 2
    x = (row // 2) % 4
    y = (row // 8) % 4
    z = (row // 32) * 4 + z_lo
    return row, z_lo, core, x, y, z


def partners():
    row, z_lo, core, x, y, z = coords()
    sibling = [(row + 1 - 2 * core, z_lo, 1 - core)]
    xs = [(row + ((x + d) % 4 - x) * 2, z_lo, (x + d) % 4) for d in (2, 1, 3)]
    ys = [(row + ((y + d) % 4 - y) * 8, z_lo, (y + d) % 4) for d in (2, 1, 3)]
    zs = []
    for d in (4, 3, 5, 2, 6, 1, 7):
        k = (z + d) % 8
        zs.append((row + (k // 4 - z // 4) * 32, k % 4, k))
    return sibling, xs, ys, zs


def remote(src, dst, send, recv, dev):
    return pltpu.make_async_remote_copy(
        src_ref=src, dst_ref=dst, send_sem=send, recv_sem=recv,
        device_id=(dev[0], dev[1]), device_id_type=MESH)


BATCH, HALF, PART = 256, 128, 32


def line_sum(own, line, at):
    total = own
    for dev in line:
        total = total + at(dev[2]).astype(F32)
    return total


def make_reduce(g, bias, gout, bout, rc, s1, r1, t1, r2, zin, rz, zfull, bc, bx, by, bz,
                send, recv):
    row, z_lo, core, x, y, z = coords()
    sibling, xs, ys, zs = partners()
    first = ((xs, x), (ys, y))
    second = ((ys, y), (xs, x))
    sent = []
    drained = [0]

    def go(src, dst, rsem, dev):
        c = remote(src, dst, send.at[len(sent)], recv.at[rsem], dev)
        c.start()
        sent.append(c)

    def land(dst, rsem):
        remote(dst, dst, send.at[0], recv.at[rsem], sibling[0]).wait_recv()

    mine = pl.ds(pl.multiple_of(core * 512, 512), 512)
    other = pl.ds(pl.multiple_of((1 - core) * 512, 512), 512)

    def batch(b):
        return pl.ds(b * BATCH, BATCH)

    def part(b, h, j):
        return pl.ds(pl.multiple_of(b * BATCH + h * HALF + j * PART, PART), PART)

    def block(j):
        return pl.ds(pl.multiple_of(core * 512 + j * 128, 128), 128)

    def n_core(b):
        return b

    def n_s1(b, h, j):
        return 3 + b * 8 + h * 4 + j

    def n_s2(b, h, j):
        return 27 + b * 8 + h * 4 + j

    def n_z(b, j):
        return 51 + b * 8 + j

    def n_zback(b, j):
        return 75 + b * 8 + j

    def n_s2back(b, h, j):
        return 99 + b * 8 + h * 4 + j

    def n_s1back(b, h, j):
        return 123 + b * 8 + h * 4 + j

    def n_coreback(b, h, j):
        return 147 + b * 8 + h * 4 + j

    n_bias = 171

    def pair(b):
        go(g.at[batch(b), other], rc.at[batch(b), :], n_core(b), sibling[0])

    def pair_bias():
        go(bias, bc, n_bias, sibling[0])

    def over_first(b):
        land(rc.at[batch(b), :], n_core(b))
        for h, (line, me) in enumerate(first):
            s1[pl.ds(b * BATCH + h * HALF, HALF), :] = (
                g[pl.ds(b * BATCH + h * HALF, HALF), mine].astype(F32)
                + rc[pl.ds(b * BATCH + h * HALF, HALF), :].astype(F32)
            ).astype(BF)
        for n in range(3):
            for h, (line, me) in enumerate(first):
                dev = line[n]
                go(s1.at[part(b, h, dev[2]), :], r1.at[b, h, me], n_s1(b, h, me), dev)

    def bias_first():
        land(bc, n_bias)
        bx[x] = bias[...] + bc[...]
        for dev in xs:
            go(bx.at[x], bx.at[x], n_bias + 1 + x, dev)

    def over_second(b):
        for h, (line, me) in enumerate(first):
            for dev in line:
                land(r1.at[b, h, dev[2]], n_s1(b, h, dev[2]))
            total = line_sum(s1[part(b, h, me), :].astype(F32), line, lambda j: r1[b, h, j])
            t1[b, h] = total.astype(BF)
            for dev in second[h][0]:
                lanes = pl.ds(pl.multiple_of(dev[2] * 128, 128), 128)
                m = second[h][1]
                go(t1.at[b, h, :, lanes], r2.at[b, h, m], n_s2(b, h, m), dev)

    def bias_second():
        for dev in xs:
            land(bx.at[dev[2]], n_bias + 1 + dev[2])
        by[y] = bx[0] + bx[1] + bx[2] + bx[3]
        for dev in ys:
            go(by.at[y], by.at[y], n_bias + 5 + y, dev)

    def over_z(b):
        for h, (line, me) in enumerate(second):
            for dev in line:
                land(r2.at[b, h, dev[2]], n_s2(b, h, dev[2]))
            own = t1[b, h, :, pl.ds(pl.multiple_of(me * 128, 128), 128)].astype(F32)
            total = line_sum(own, line, lambda j: r2[b, h, j])
            zin[b, h * 4 : h * 4 + 4] = total.reshape(4, 8, 128)
        for dev in zs:
            go(zin.at[b, dev[2]], rz.at[b, z], n_z(b, z), dev)

    def bias_z():
        for dev in ys:
            land(by.at[dev[2]], n_bias + 5 + dev[2])
        bz[z] = by[0] + by[1] + by[2] + by[3]
        for dev in zs:
            go(bz.at[z], bz.at[z], n_bias + 9 + z, dev)

    def back_z(b):
        for dev in zs:
            land(rz.at[b, dev[2]], n_z(b, dev[2]))
        zfull[b, z] = line_sum(zin[b, z], zs, lambda j: rz[b, j])
        for dev in zs:
            go(zfull.at[b, z], zfull.at[b, z], n_zback(b, z), dev)

    def bias_end():
        for dev in zs:
            land(bz.at[dev[2]], n_bias + 9 + dev[2])
        bout[...] = ((bz[0] + bz[1]) + (bz[2] + bz[3])) + ((bz[4] + bz[5]) + (bz[6] + bz[7]))

    def back_second(b):
        for dev in zs:
            land(zfull.at[b, dev[2]], n_zback(b, dev[2]))
        for h, (line, me) in enumerate(second):
            rows = part(b, h, first[h][1])
            gout[rows, block(me)] = zfull[b, h * 4 : h * 4 + 4].reshape(PART, 128).astype(BF)
            for dev in line:
                go(gout.at[rows, block(me)], gout.at[rows, block(me)], n_s2back(b, h, me), dev)

    def back_first(b):
        for h, (line, me) in enumerate(second):
            own = first[h][1]
            rows = part(b, h, own)
            for dev in line:
                land(gout.at[rows, block(dev[2])], n_s2back(b, h, dev[2]))
            for dev in first[h][0]:
                go(gout.at[rows, mine], gout.at[rows, mine], n_s1back(b, h, own), dev)
            go(gout.at[rows, mine], gout.at[rows, mine], n_coreback(b, h, own), sibling[0])

    def back_pair(b):
        for h, (line, me) in enumerate(first):
            for dev in line:
                rows = part(b, h, dev[2])
                land(gout.at[rows, mine], n_s1back(b, h, dev[2]))
                go(gout.at[rows, mine], gout.at[rows, mine], n_coreback(b, h, dev[2]), sibling[0])

    def back_end(b):
        for h in range(2):
            for j in range(4):
                land(gout.at[part(b, h, j), other], n_coreback(b, h, j))

    def drain(count):
        for c in sent[drained[0] : count]:
            c.wait_send()
        drained[0] = max(count, drained[0])

    def finish():
        drain(len(sent))

    def started():
        return len(sent)

    return dict(pair=pair, pair_bias=pair_bias, over_first=over_first, bias_first=bias_first,
                over_second=over_second, bias_second=bias_second, over_z=over_z, bias_z=bias_z,
                back_z=back_z, bias_end=bias_end, back_second=back_second, back_first=back_first,
                back_pair=back_pair, back_end=back_end, finish=finish,
                drain=drain, started=started)


AR_SCRATCH = [
    pltpu.VMEM((768, 512), BF),
    pltpu.VMEM((768, 512), BF),
    pltpu.VMEM((3, 2, 4, 32, 512), BF),
    pltpu.VMEM((3, 2, 32, 512), BF),
    pltpu.VMEM((3, 2, 4, 32, 128), BF),
    pltpu.VMEM((3, 8, 8, 128), F32),
    pltpu.VMEM((3, 8, 8, 128), F32),
    pltpu.VMEM((3, 8, 8, 128), F32),
    pltpu.VMEM((16, 128), F32),
    pltpu.VMEM((4, 16, 128), F32),
    pltpu.VMEM((4, 16, 128), F32),
    pltpu.VMEM((8, 16, 128), F32),
    pltpu.SemaphoreType.DMA((184,)),
    pltpu.SemaphoreType.DMA((192,)),
]


def greet(devs):
    barrier = pltpu.get_barrier_semaphore()
    for dev in devs:
        pl.semaphore_signal(barrier, inc=1, device_id=(dev[0], dev[1]), device_id_type=MESH)
    pl.semaphore_wait(barrier, len(devs))


SCALE_TILE = 0.25 / math.sqrt(512)
C0 = math.sqrt(2.0 / math.pi)
C1 = C0 * 0.044715
T_RHS = (((1,), (1,)), ((), ()))


def mm(a, b):
    return jnp.dot(a, b, preferred_element_type=F32)


def mm_t(a, b):
    return lax.dot_general(a, b, T_RHS, preferred_element_type=F32)


def ds256(i):
    return pl.ds(pl.multiple_of(i * 256, 256), 256)


SENDS = {0: (0,), 1: (1,), 2: (2,), 3: (7, 3, 6), "back_z": (5, 4)}

REST = {"over_z": (0, 4)}


def neighbours():
    row, z_lo, core, x, y, z = coords()
    here = row * 4 + z_lo
    right = (here + 1) % 256
    left = (here + 255) % 256
    return here, (left // 4, left % 4), (right // 4, right % 4)


def layer_kernel(
    cols, x_hbm, tw_hbm, ws_hbm, wn_hbm, bh, wo_hbm, bo, cot_hbm,
    embed_hbm, gradf_hbm, gwo_hbm, gws_hbm, gwn_hbm, bout,
    embed, gradf, gout, gwo,
    win, tw, ws, wn, wo, cot, dup, dense, pre, dact, agg0, xt, ct, at,
    hid, dh, da_t, bsum, own, lo, hi, lo_b, hi_b, from_r, from_l, g, bias,
    in_sem, out_sem, halo_send, halo_recv, *ar,
):
    here, left, right = neighbours()
    sibling, xs, ys, zs = partners()

    loads = []
    for n, (src, dst) in enumerate((
        (tw_hbm, tw), (x_hbm, win.at[pl.ds(1024, 1024), :]), (cot_hbm, cot),
        (ws_hbm, ws), (wo_hbm, wo), (wn_hbm, wn),
    )):
        c = pltpu.make_async_copy(src, dst, in_sem.at[n])
        c.start()
        loads.append(c)
    greet([left, right] + sibling + xs + ys + zs)

    halo = []
    writes = []

    def write(src, dst):
        c = pltpu.make_async_copy(src, dst, out_sem.at[len(writes)])
        c.start()
        writes.append(c)

    def halo_copy(src, dst, n, dev):
        c = remote(src, dst, halo_send.at[n], halo_recv.at[n], dev)
        c.start()
        halo.append(c)

    def halo_wait(n):
        first, size = (256 * n, 256)
        for f, size_f, n_f in highs:
            if n_f == n:
                first, size = 2048 + f, size_f
        dst = win.at[pl.ds(first, size), :]
        remote(dst, dst, halo_send.at[n], halo_recv.at[n], left).wait_recv()

    for i in range(4):
        rows = pl.ds(256 * i, 256)
        halo_copy(x_hbm.at[rows, :], win.at[rows, :], i, right)
    highs = ((0, 256, 4), (256, 256, 5), (512, 256, 6), (768, 128, 7), (896, 128, 16))
    for first, size, n in highs:
        halo_copy(x_hbm.at[pl.ds(first, size), :], win.at[pl.ds(2048 + first, size), :], n, left)

    def build_dense():
        lane = lax.broadcasted_iota(jnp.int32, (64, 128), 1)
        half = lax.broadcasted_iota(jnp.int32, (1, 128), 1) // 64

        @pl.loop(0, 16)
        def _(p):
            c = p // 4
            rows = pl.ds(pl.multiple_of((p % 4) * 64, 64), 64)
            base = here * 16 - 16 + 4 * c
            for q in range(4):
                u = tw[p, :, 128 * q : 128 * q + 128].astype(F32) * SCALE_TILE
                u = u.astype(BF).astype(F32)
                r = pltpu.roll(u, 64, 1)
                dup[2 * q] = jnp.where(lane < 64, u, r)
                dup[2 * q + 1] = jnp.where(lane < 64, r, u)
            spot = [cols[s, p] - base for s in range(8)]

            @pl.loop(0, 18)
            def _(j):
                total = jnp.zeros((64, 128), F32)
                for s in range(8):
                    hit = jnp.where(half == spot[s] - 2 * j, 1.0, 0.0).astype(F32)
                    total = total + dup[s] * hit
                dense[c, rows, pl.ds(pl.multiple_of(j * 128, 128), 128)] = total.astype(BF)

    def local_part():
        bsum[...] = jnp.zeros_like(bsum)

        @pl.loop(0, 4)
        def _(c):
            rows = ds256(c)
            mine = pl.ds(pl.multiple_of(1024 + c * 256, 256), 256)
            xc = win[mine, :]
            cc = cot[rows, :]
            xt[:, rows] = xc.T
            ct[:, rows] = cc.T
            bsum[:, 1024:1280] += jnp.sum(cc.astype(F32).reshape(32, 8, 256), axis=0)
            for n in range(4):
                n4 = slice(256 * n, 256 * n + 256)
                pre[rows, n4] = mm(xc, ws[:, n4]) + bh[:, n4]
                dact[rows, n4] = mm_t(cc, wo[n4, :])
            total = jnp.zeros((256, 256), F32)
            for t in range(4):
                total = total + mm(dense[c, :, ds256(4 + t - c)], win[1024 + 256 * t : 1280 + 256 * t, :])
            agg0[rows, :] = total

    def low_part():
        for c in range(4):
            rows = slice(256 * c, 256 * c + 256)
            total = agg0[rows, :]
            for t in range(c, 4):
                total = total + mm(dense[c, :, 256 * (t - c) : 256 * (t - c) + 256], win[256 * t : 256 * t + 256, :])
            agg0[rows, :] = total

    def adjoint_round(n):
        j = n % 4
        src, buf = ((lo, lo_b), (hi, hi_b))[n // 4]
        buf[j] = src[:, 256 * j : 256 * j + 256].astype(BF)

    def adjoint_send(pieces):
        for n in pieces:
            j = n % 4
            buf, dst, dev = ((lo_b, from_r, left), (hi_b, from_l, right))[n // 4]
            halo_copy(buf.at[j], dst.at[j], 8 + n, dev)

    def chunk(c, top=0, m=256, last=256):
        r4 = slice(256 * c + top, 256 * c + top + m)
        total = agg0[r4, :]
        for t in range(c + 1):
            b = 256 * (8 + t - c)
            k = last if t == c else 256
            total = total + mm(dense[c, top : top + m, b : b + k], win[2048 + 256 * t : 2048 + 256 * t + k, :])
        ag = total.astype(BF)
        for n in range(4):
            n4 = slice(256 * n, 256 * n + 256)
            pre[r4, n4] += mm(ag, wn[:, n4])
        at[:, r4] = ag.T

        @pl.loop(0, m // 32)
        def _(i):
            r = pl.ds(pl.multiple_of(c * 256 + top + i * 32, 32), 32)
            for n in range(4):
                n4 = slice(256 * n, 256 * n + 256)
                v = pre[r, n4]
                u = v * v
                a = 0.5 * jnp.tanh(v * (C0 + C1 * u)) + 0.5
                h = v * a
                hid[r, n4] = h.astype(BF)
                slope = a + h * ((2.0 * C0) + (6.0 * C1) * u) * (1.0 - a)
                d = (dact[r, n4] * slope).astype(BF)
                dh[r, n4] = d
                bsum[:, n4] += jnp.sum(d.astype(F32).reshape(4, 8, 256), axis=0)

    def adjoint(c):
        r4 = slice(256 * c, 256 * c + 256)
        da = mm_t(wn[...], dh[r4, :]).astype(BF)
        da_t[c] = da
        for j in range(c, 4):
            part = mm(da, dense[c, :, 256 * (j - c) : 256 * (j - c) + 256])
            j4 = slice(256 * j, 256 * j + 256)
            lo[:, j4] = part if c == 0 else lo[:, j4] + part
            if j == c:
                adjoint_round(j)
        for j in range(c + 1):
            b = 256 * (8 + j - c)
            part = mm(da, dense[c, :, b : b + 256])
            j4 = slice(256 * j, 256 * j + 256)
            hi[:, j4] = part if c == j else hi[:, j4] + part
            if c == 3:
                adjoint_round(4 + j)

    def weight_grad(b):
        left_side, right_side = ((ct, hid), (xt, dh), (at, dh))[b]
        for n in range(4):
            n4 = slice(256 * n, 256 * n + 256)
            g[256 * b : 256 * b + 256, n4] = mm(left_side[...], right_side[:, n4]).astype(BF)

    def bias_grads():
        sums = jnp.sum(bsum[...], axis=0, keepdims=True)
        for n in range(10):
            bias[n : n + 1, :] = sums[:, 128 * n : 128 * n + 128]
        bias[10:16, :] = jnp.zeros((6, 128), F32)

    def local_rest(first, last):
        @pl.loop(first, last)
        def _(c):
            rows = ds256(c)
            embed[rows, :] = (mm(hid[rows, :], wo[...]) + bo[...]).astype(BF)
            total = jnp.zeros((256, 256), F32)
            for b in range(4):
                total = total + mm(da_t[b], dense[b, :, ds256(4 + c - b)])
            own[rows, :] = mm_t(dh[rows, :], ws[...]) + total.T

    def last_sum():
        for j in (0, 1, 2, 3):
            for m, dst in ((j, from_r), (4 + j, from_l)):
                remote(dst.at[j], dst.at[j], halo_send.at[8 + m], halo_recv.at[8 + m], left).wait_recv()
            rows = slice(256 * j, 256 * j + 256)
            outer = from_l[j].astype(F32) + from_r[j].astype(F32)
            gradf[rows, :] = (own[rows, :] + outer.T).astype(BF)

    loads[0].wait()
    build_dense()
    for c in loads[1:]:
        c.wait()
    local_part()
    for n in range(4):
        halo_wait(n)
    low_part()
    red = make_reduce(g, bias, gout, bout, *ar)
    for c in range(4):
        halo_wait(4 + c)
        if c < 3:
            chunk(c)
        else:
            chunk(c, 0, 128, 128)
            halo_wait(16)
            chunk(c, 128, 128, 256)
            weight_grad(0)
            red["pair"](0)
        adjoint(c)
        adjoint_send(SENDS[c])
    red["over_first"](0)
    weight_grad(1)
    red["pair"](1)
    weight_grad(2)
    red["pair"](2)
    red["over_first"](1)
    bias_grads()
    red["pair_bias"]()
    red["over_first"](2)
    red["bias_first"]()
    for stage in ("over_second", "over_z", "back_z", "back_second", "back_first"):
        before = red["started"]()
        for b in range(3):
            red[stage](b)
        adjoint_send(SENDS.get(stage, ()))
        if stage in REST:
            local_rest(*REST[stage])
            if REST[stage][1] == 4:
                write(embed, embed_hbm)
        tail = {"over_second": "bias_second", "over_z": "bias_z", "back_z": "bias_end"}.get(stage)
        if tail is not None:
            red[tail]()
        red["drain"](before)
    last_sum()
    write(gradf, gradf_hbm)
    before = red["started"]()
    red["back_pair"](0)
    red["back_pair"](1)
    red["back_end"](0)
    for n in range(4):
        n4 = slice(256 * n, 256 * n + 256)
        gwo[n4, :] = gout[0:256, n4].T
    write(gwo, gwo_hbm)
    red["back_pair"](2)
    red["drain"](before)
    red["back_end"](1)
    write(gout.at[pl.ds(256, 256), :], gws_hbm)
    red["back_end"](2)
    write(gout.at[pl.ds(512, 256), :], gwn_hbm)
    red["finish"]()
    for c in halo:
        c.wait_send()
    for c in writes:
        c.wait()


LAYER_SCRATCH = [
    pltpu.VMEM((1024, 256), BF),
    pltpu.VMEM((1024, 256), BF),
    pltpu.VMEM((768, 1024), BF),
    pltpu.VMEM((1024, 256), BF),
    pltpu.VMEM((3072, 256), BF),
    pltpu.VMEM((16, 64, 512), jnp.int32),
    pltpu.VMEM((256, 1024), BF),
    pltpu.VMEM((256, 1024), BF),
    pltpu.VMEM((1024, 256), BF),
    pltpu.VMEM((1024, 256), BF),
    pltpu.VMEM((8, 64, 128), F32),
    pltpu.VMEM((4, 256, 2304), BF),
    pltpu.VMEM((1024, 1024), F32),
    pltpu.VMEM((1024, 1024), F32),
    pltpu.VMEM((1024, 256), F32),
    pltpu.VMEM((256, 1024), BF),
    pltpu.VMEM((256, 1024), BF),
    pltpu.VMEM((256, 1024), BF),
    pltpu.VMEM((1024, 1024), BF),
    pltpu.VMEM((1024, 1024), BF),
    pltpu.VMEM((4, 256, 256), BF),
    pltpu.VMEM((8, 1280), F32),
    pltpu.VMEM((1024, 256), F32),
    pltpu.VMEM((256, 1024), F32),
    pltpu.VMEM((256, 1024), F32),
    pltpu.VMEM((4, 256, 256), BF),
    pltpu.VMEM((4, 256, 256), BF),
    pltpu.VMEM((4, 256, 256), BF),
    pltpu.VMEM((4, 256, 256), BF),
    pltpu.VMEM((768, 1024), BF),
    pltpu.VMEM((16, 128), F32),
    pltpu.SemaphoreType.DMA((6,)),
    pltpu.SemaphoreType.DMA((5,)),
    pltpu.SemaphoreType.DMA((17,)),
    pltpu.SemaphoreType.DMA((17,)),
]


def scale_kernel(embed, gradf, gws, gwn, bias, gwo, embed_o, gradf_o, gws_o, gwn_o, bh_o, gwo_o, bo_o):
    scale = 1.0 / math.sqrt(1024 * 256)
    embed_o[...] = embed[...]
    gradf_o[...] = gradf[...]
    gws_o[...] = gws[...].astype(F32) * scale
    gwn_o[...] = gwn[...].astype(F32) * scale
    gwo_o[...] = gwo[...].astype(F32) * scale
    bh_o[...] = bias[0:8, :] * scale
    bo_o[...] = bias[8:10, :] * scale


def scaled_outputs(embed, gradf, gws, gwn, bias, gwo):
    steps = 2
    tall = pl.BlockSpec((1024 // steps, 256), lambda i: (i, 0))
    wide = pl.BlockSpec((256 // steps, 1024), lambda i: (i, 0))

    def whole(rows):
        return pl.BlockSpec((rows, 128), lambda i: (0, 0))

    embed, gradf, gws, gwn, bh, gwo, bo = pl.pallas_call(
        scale_kernel,
        grid=(steps,),
        out_shape=(
            jax.ShapeDtypeStruct((1024, 256), BF),
            jax.ShapeDtypeStruct((1024, 256), BF),
            jax.ShapeDtypeStruct((256, 1024), F32),
            jax.ShapeDtypeStruct((256, 1024), F32),
            jax.ShapeDtypeStruct((8, 128), F32),
            jax.ShapeDtypeStruct((1024, 256), F32),
            jax.ShapeDtypeStruct((2, 128), F32),
        ),
        in_specs=[tall, tall, wide, wide, whole(16), tall],
        out_specs=(tall, tall, wide, wide, whole(8), tall, whole(2)),
        name="scaled_outputs",
    )(embed, gradf, gws, gwn, bias, gwo)
    return embed, gradf, gws, gwn, bh.reshape(1024), gwo, bo.reshape(256)


def local(
    node_features, tile_cols, tile_weights, w_self, w_neigh, bias_hidden, w_out, bias_out, cotangent
):
    vm = pl.BlockSpec(memory_space=pltpu.VMEM)
    hbm = pl.BlockSpec(memory_space=pl.ANY)
    sm = pl.BlockSpec(memory_space=pltpu.SMEM)
    embed, grad_features, gwo, gws, gwn, bias = pl.pallas_call(
        layer_kernel,
        out_shape=(
            jax.ShapeDtypeStruct((1024, 256), BF),
            jax.ShapeDtypeStruct((1024, 256), BF),
            jax.ShapeDtypeStruct((1024, 256), BF),
            jax.ShapeDtypeStruct((256, 1024), BF),
            jax.ShapeDtypeStruct((256, 1024), BF),
            jax.ShapeDtypeStruct((16, 128), F32),
        ),
        in_specs=[sm, hbm, hbm, hbm, hbm, vm, hbm, vm, hbm],
        out_specs=(hbm, hbm, hbm, hbm, hbm, vm),
        scratch_shapes=LAYER_SCRATCH + AR_SCRATCH,
        compiler_params=pltpu.CompilerParams(
            collective_id=0, has_side_effects=True, vmem_limit_bytes=60 << 20
        ),
        name="layer",
    )(
        tile_cols.T, node_features, tile_weights, w_self, w_neigh,
        bias_hidden.reshape(1, 1024), w_out, bias_out.reshape(1, 256), cotangent,
    )
    return scaled_outputs(embed, grad_features, gws, gwn, bias, gwo)


def solution(mesh):
    in_specs = (
        P(("row", "col"), None),
        P(("row", "col"), None),
        P(("row", "col"), None, None),
        P(),
        P(),
        P(),
        P(),
        P(),
        P(("row", "col"), None),
    )
    out_specs = (P(("row", "col"), None), P(("row", "col"), None), P(), P(), P(), P(), P())
    return jax.shard_map(local, mesh=mesh, in_specs=in_specs, out_specs=out_specs, check_vma=False)
```

```python
import math

import jax
import jax.numpy as jnp
from jax import lax
from jax.experimental import pallas as pl
from jax.experimental.pallas import tpu as pltpu
from jax.sharding import PartitionSpec as P

MESH = pl.DeviceIdType.MESH
BF, F32 = jnp.bfloat16, jnp.float32


def coords():
    row, z_lo = lax.axis_index("row"), lax.axis_index("col")
    core = row % 2
    x = (row // 2) % 4
    y = (row // 8) % 4
    z = (row // 32) * 4 + z_lo
    return row, z_lo, core, x, y, z


def partners():
    row, z_lo, core, x, y, z = coords()
    sibling = [(row + 1 - 2 * core, z_lo, 1 - core)]
    xs = [(row + ((x + d) % 4 - x) * 2, z_lo, (x + d) % 4) for d in (2, 1, 3)]
    ys = [(row + ((y + d) % 4 - y) * 8, z_lo, (y + d) % 4) for d in (2, 1, 3)]
    zs = []
    for d in (4, 3, 5, 2, 6, 1, 7):
        k = (z + d) % 8
        zs.append((row + (k // 4 - z // 4) * 32, k % 4, k))
    return sibling, xs, ys, zs


def remote(src, dst, send, recv, dev):
    return pltpu.make_async_remote_copy(
        src_ref=src, dst_ref=dst, send_sem=send, recv_sem=recv,
        device_id=(dev[0], dev[1]), device_id_type=MESH)


BATCH, HALF, PART = 256, 128, 32


def line_sum(own, line, at):
    total = own
    for dev in line:
        total = total + at(dev[2]).astype(F32)
    return total


def make_reduce(g, bias, gout, bout, rc, s1, r1, t1, r2, zin, rz, zfull, bc, bx, by, bz,
                send, recv):
    row, z_lo, core, x, y, z = coords()
    sibling, xs, ys, zs = partners()
    first = ((xs, x), (ys, y))
    second = ((ys, y), (xs, x))
    sent = []
    drained = [0]

    def go(src, dst, rsem, dev):
        c = remote(src, dst, send.at[len(sent)], recv.at[rsem], dev)
        c.start()
        sent.append(c)

    def land(dst, rsem):
        remote(dst, dst, send.at[0], recv.at[rsem], sibling[0]).wait_recv()

    mine = pl.ds(pl.multiple_of(core * 512, 512), 512)
    other = pl.ds(pl.multiple_of((1 - core) * 512, 512), 512)

    def batch(b):
        return pl.ds(b * BATCH, BATCH)

    def part(b, h, j):
        return pl.ds(pl.multiple_of(b * BATCH + h * HALF + j * PART, PART), PART)

    def block(j):
        return pl.ds(pl.multiple_of(core * 512 + j * 128, 128), 128)

    def n_core(b):
        return b

    def n_s1(b, h, j):
        return 3 + b * 8 + h * 4 + j

    def n_s2(b, h, j):
        return 27 + b * 8 + h * 4 + j

    def n_z(b, j):
        return 51 + b * 8 + j

    def n_zback(b, j):
        return 75 + b * 8 + j

    def n_s2back(b, h, j):
        return 99 + b * 8 + h * 4 + j

    def n_s1back(b, h, j):
        return 123 + b * 8 + h * 4 + j

    def n_coreback(b, h, j):
        return 147 + b * 8 + h * 4 + j

    n_bias = 171

    def pair(b):
        go(g.at[batch(b), other], rc.at[batch(b), :], n_core(b), sibling[0])

    def pair_bias():
        go(bias, bc, n_bias, sibling[0])

    def over_first(b):
        land(rc.at[batch(b), :], n_core(b))
        for h, (line, me) in enumerate(first):
            s1[pl.ds(b * BATCH + h * HALF, HALF), :] = (
                g[pl.ds(b * BATCH + h * HALF, HALF), mine].astype(F32)
                + rc[pl.ds(b * BATCH + h * HALF, HALF), :].astype(F32)
            ).astype(BF)
        for n in range(3):
            for h, (line, me) in enumerate(first):
                dev = line[n]
                go(s1.at[part(b, h, dev[2]), :], r1.at[b, h, me], n_s1(b, h, me), dev)

    def bias_first():
        land(bc, n_bias)
        bx[x] = bias[...] + bc[...]
        for dev in xs:
            go(bx.at[x], bx.at[x], n_bias + 1 + x, dev)

    def over_second(b):
        for h, (line, me) in enumerate(first):
            for dev in line:
                land(r1.at[b, h, dev[2]], n_s1(b, h, dev[2]))
            total = line_sum(s1[part(b, h, me), :].astype(F32), line, lambda j: r1[b, h, j])
            t1[b, h] = total.astype(BF)
            for dev in second[h][0]:
                lanes = pl.ds(pl.multiple_of(dev[2] * 128, 128), 128)
                m = second[h][1]
                go(t1.at[b, h, :, lanes], r2.at[b, h, m], n_s2(b, h, m), dev)

    def bias_second():
        for dev in xs:
            land(bx.at[dev[2]], n_bias + 1 + dev[2])
        by[y] = bx[0] + bx[1] + bx[2] + bx[3]
        for dev in ys:
            go(by.at[y], by.at[y], n_bias + 5 + y, dev)

    def over_z(b):
        for h, (line, me) in enumerate(second):
            for dev in line:
                land(r2.at[b, h, dev[2]], n_s2(b, h, dev[2]))
            own = t1[b, h, :, pl.ds(pl.multiple_of(me * 128, 128), 128)].astype(F32)
            total = line_sum(own, line, lambda j: r2[b, h, j])
            zin[b, h * 4 : h * 4 + 4] = total.reshape(4, 8, 128)
        for dev in zs:
            go(zin.at[b, dev[2]], rz.at[b, z], n_z(b, z), dev)

    def bias_z():
        for dev in ys:
            land(by.at[dev[2]], n_bias + 5 + dev[2])
        bz[z] = by[0] + by[1] + by[2] + by[3]
        for dev in zs:
            go(bz.at[z], bz.at[z], n_bias + 9 + z, dev)

    def back_z(b):
        for dev in zs:
            land(rz.at[b, dev[2]], n_z(b, dev[2]))
        zfull[b, z] = line_sum(zin[b, z], zs, lambda j: rz[b, j])
        for dev in zs:
            go(zfull.at[b, z], zfull.at[b, z], n_zback(b, z), dev)

    def bias_end():
        for dev in zs:
            land(bz.at[dev[2]], n_bias + 9 + dev[2])
        bout[...] = ((bz[0] + bz[1]) + (bz[2] + bz[3])) + ((bz[4] + bz[5]) + (bz[6] + bz[7]))

    def back_second(b):
        for dev in zs:
            land(zfull.at[b, dev[2]], n_zback(b, dev[2]))
        for h, (line, me) in enumerate(second):
            rows = part(b, h, first[h][1])
            gout[rows, block(me)] = zfull[b, h * 4 : h * 4 + 4].reshape(PART, 128).astype(BF)
            for dev in line:
                go(gout.at[rows, block(me)], gout.at[rows, block(me)], n_s2back(b, h, me), dev)

    def back_first(b):
        for h, (line, me) in enumerate(second):
            own = first[h][1]
            rows = part(b, h, own)
            for dev in line:
                land(gout.at[rows, block(dev[2])], n_s2back(b, h, dev[2]))
            for dev in first[h][0]:
                go(gout.at[rows, mine], gout.at[rows, mine], n_s1back(b, h, own), dev)
            go(gout.at[rows, mine], gout.at[rows, mine], n_coreback(b, h, own), sibling[0])

    def back_pair(b):
        for h, (line, me) in enumerate(first):
            for dev in line:
                rows = part(b, h, dev[2])
                land(gout.at[rows, mine], n_s1back(b, h, dev[2]))
                go(gout.at[rows, mine], gout.at[rows, mine], n_coreback(b, h, dev[2]), sibling[0])

    def back_end(b):
        for h in range(2):
            for j in range(4):
                land(gout.at[part(b, h, j), other], n_coreback(b, h, j))

    def drain(count):
        for c in sent[drained[0] : count]:
            c.wait_send()
        drained[0] = max(count, drained[0])

    def finish():
        drain(len(sent))

    def started():
        return len(sent)

    return dict(pair=pair, pair_bias=pair_bias, over_first=over_first, bias_first=bias_first,
                over_second=over_second, bias_second=bias_second, over_z=over_z, bias_z=bias_z,
                back_z=back_z, bias_end=bias_end, back_second=back_second, back_first=back_first,
                back_pair=back_pair, back_end=back_end, finish=finish,
                drain=drain, started=started)


AR_SCRATCH = [
    pltpu.VMEM((768, 512), BF),
    pltpu.VMEM((768, 512), BF),
    pltpu.VMEM((3, 2, 4, 32, 512), BF),
    pltpu.VMEM((3, 2, 32, 512), BF),
    pltpu.VMEM((3, 2, 4, 32, 128), BF),
    pltpu.VMEM((3, 8, 8, 128), F32),
    pltpu.VMEM((3, 8, 8, 128), F32),
    pltpu.VMEM((3, 8, 8, 128), F32),
    pltpu.VMEM((16, 128), F32),
    pltpu.VMEM((4, 16, 128), F32),
    pltpu.VMEM((4, 16, 128), F32),
    pltpu.VMEM((8, 16, 128), F32),
    pltpu.SemaphoreType.DMA((184,)),
    pltpu.SemaphoreType.DMA((192,)),
]


def greet(devs):
    barrier = pltpu.get_barrier_semaphore()
    for dev in devs:
        pl.semaphore_signal(barrier, inc=1, device_id=(dev[0], dev[1]), device_id_type=MESH)
    pl.semaphore_wait(barrier, len(devs))


SCALE_TILE = 0.25 / math.sqrt(512)
C0 = math.sqrt(2.0 / math.pi)
C1 = C0 * 0.044715
T_RHS = (((1,), (1,)), ((), ()))


def mm(a, b):
    return jnp.dot(a, b, preferred_element_type=F32)


def mm_t(a, b):
    return lax.dot_general(a, b, T_RHS, preferred_element_type=F32)


def ds256(i):
    return pl.ds(pl.multiple_of(i * 256, 256), 256)


SENDS = {0: (0,), 1: (1,), 2: (2,), 3: (7, 3, 6), "back_z": (5, 4)}

REST = {"over_z": (0, 4)}


def neighbours():
    row, z_lo, core, x, y, z = coords()
    here = row * 4 + z_lo
    right = (here + 1) % 256
    left = (here + 255) % 256
    return here, (left // 4, left % 4), (right // 4, right % 4)


def layer_kernel(
    cols, x_hbm, tw_hbm, ws_hbm, wn_hbm, bh, wo_hbm, bo, cot_hbm,
    embed_hbm, gradf_hbm, gwo_hbm, gws_hbm, gwn_hbm, bout,
    embed, gradf, gout, gwo,
    win, tw, ws, wn, wo, cot, dup, dense, pre, dact, agg0, xt, ct, at,
    hid, dh, da_t, bsum, own, lo, hi, lo_b, hi_b, from_r, from_l, g, bias,
    in_sem, out_sem, halo_send, halo_recv, *ar,
):
    here, left, right = neighbours()
    sibling, xs, ys, zs = partners()

    loads = []
    for n, (src, dst) in enumerate((
        (tw_hbm, tw), (x_hbm, win.at[pl.ds(1024, 1024), :]), (cot_hbm, cot),
        (ws_hbm, ws), (wo_hbm, wo), (wn_hbm, wn),
    )):
        c = pltpu.make_async_copy(src, dst, in_sem.at[n])
        c.start()
        loads.append(c)
    greet([left, right] + sibling + xs + ys + zs)

    halo = []
    writes = []

    def write(src, dst):
        c = pltpu.make_async_copy(src, dst, out_sem.at[len(writes)])
        c.start()
        writes.append(c)

    def halo_copy(src, dst, n, dev):
        c = remote(src, dst, halo_send.at[n], halo_recv.at[n], dev)
        c.start()
        halo.append(c)

    def halo_wait(n):
        first, size = (256 * n, 256)
        for f, size_f, n_f in highs:
            if n_f == n:
                first, size = 2048 + f, size_f
        dst = win.at[pl.ds(first, size), :]
        remote(dst, dst, halo_send.at[n], halo_recv.at[n], left).wait_recv()

    for i in range(4):
        rows = pl.ds(256 * i, 256)
        halo_copy(x_hbm.at[rows, :], win.at[rows, :], i, right)
    highs = ((0, 256, 4), (256, 256, 5), (512, 256, 6), (768, 128, 7), (896, 128, 16))
    for first, size, n in highs:
        halo_copy(x_hbm.at[pl.ds(first, size), :], win.at[pl.ds(2048 + first, size), :], n, left)

    def build_dense():
        lane = lax.broadcasted_iota(jnp.int32, (64, 128), 1)
        half = lax.broadcasted_iota(jnp.int32, (1, 128), 1) // 64

        @pl.loop(0, 16)
        def _(p):
            c = p // 4
            rows = pl.ds(pl.multiple_of((p % 4) * 64, 64), 64)
            base = here * 16 - 16 + 4 * c
            for q in range(4):
                u = tw[p, :, 128 * q : 128 * q + 128].astype(F32) * SCALE_TILE
                u = u.astype(BF).astype(F32)
                r = pltpu.roll(u, 64, 1)
                dup[2 * q] = jnp.where(lane < 64, u, r)
                dup[2 * q + 1] = jnp.where(lane < 64, r, u)
            spot = [cols[s, p] - base for s in range(8)]

            @pl.loop(0, 18)
            def _(j):
                total = jnp.zeros((64, 128), F32)
                for s in range(8):
                    hit = jnp.where(half == spot[s] - 2 * j, 1.0, 0.0).astype(F32)
                    total = total + dup[s] * hit
                dense[c, rows, pl.ds(pl.multiple_of(j * 128, 128), 128)] = total.astype(BF)

    def local_part():
        bsum[...] = jnp.zeros_like(bsum)

        @pl.loop(0, 4)
        def _(c):
            rows = ds256(c)
            mine = pl.ds(pl.multiple_of(1024 + c * 256, 256), 256)
            xc = win[mine, :]
            cc = cot[rows, :]
            xt[:, rows] = xc.T
            ct[:, rows] = cc.T
            bsum[:, 1024:1280] += jnp.sum(cc.astype(F32).reshape(32, 8, 256), axis=0)
            for n in range(4):
                n4 = slice(256 * n, 256 * n + 256)
                pre[rows, n4] = mm(xc, ws[:, n4]) + bh[:, n4]
                dact[rows, n4] = mm_t(cc, wo[n4, :])
            total = jnp.zeros((256, 256), F32)
            for t in range(4):
                total = total + mm(dense[c, :, ds256(4 + t - c)], win[1024 + 256 * t : 1280 + 256 * t, :])
            agg0[rows, :] = total

    def low_part():
        for c in range(4):
            rows = slice(256 * c, 256 * c + 256)
            total = agg0[rows, :]
            for t in range(c, 4):
                total = total + mm(dense[c, :, 256 * (t - c) : 256 * (t - c) + 256], win[256 * t : 256 * t + 256, :])
            agg0[rows, :] = total

    def adjoint_round(n):
        j = n % 4
        src, buf = ((lo, lo_b), (hi, hi_b))[n // 4]
        buf[j] = src[:, 256 * j : 256 * j + 256].astype(BF)

    def adjoint_send(pieces):
        for n in pieces:
            j = n % 4
            buf, dst, dev = ((lo_b, from_r, left), (hi_b, from_l, right))[n // 4]
            halo_copy(buf.at[j], dst.at[j], 8 + n, dev)

    def chunk(c, top=0, m=256, last=256):
        r4 = slice(256 * c + top, 256 * c + top + m)
        total = agg0[r4, :]
        for t in range(c + 1):
            b = 256 * (8 + t - c)
            k = last if t == c else 256
            total = total + mm(dense[c, top : top + m, b : b + k], win[2048 + 256 * t : 2048 + 256 * t + k, :])
        ag = total.astype(BF)
        for n in range(4):
            n4 = slice(256 * n, 256 * n + 256)
            pre[r4, n4] += mm(ag, wn[:, n4])
        at[:, r4] = ag.T

        @pl.loop(0, m // 32)
        def _(i):
            r = pl.ds(pl.multiple_of(c * 256 + top + i * 32, 32), 32)
            for n in range(4):
                n4 = slice(256 * n, 256 * n + 256)
                v = pre[r, n4]
                u = v * v
                a = 0.5 * jnp.tanh(v * (C0 + C1 * u)) + 0.5
                h = v * a
                hid[r, n4] = h.astype(BF)
                slope = a + h * ((2.0 * C0) + (6.0 * C1) * u) * (1.0 - a)
                d = (dact[r, n4] * slope).astype(BF)
                dh[r, n4] = d
                bsum[:, n4] += jnp.sum(d.astype(F32).reshape(4, 8, 256), axis=0)

    def adjoint(c):
        r4 = slice(256 * c, 256 * c + 256)
        da = mm_t(wn[...], dh[r4, :]).astype(BF)
        da_t[c] = da
        for j in range(c, 4):
            part = mm(da, dense[c, :, 256 * (j - c) : 256 * (j - c) + 256])
            j4 = slice(256 * j, 256 * j + 256)
            lo[:, j4] = part if c == 0 else lo[:, j4] + part
            if j == c:
                adjoint_round(j)
        for j in range(c + 1):
            b = 256 * (8 + j - c)
            part = mm(da, dense[c, :, b : b + 256])
            j4 = slice(256 * j, 256 * j + 256)
            hi[:, j4] = part if c == j else hi[:, j4] + part
            if c == 3:
                adjoint_round(4 + j)

    def weight_grad(b):
        left_side, right_side = ((ct, hid), (xt, dh), (at, dh))[b]
        for n in range(4):
            n4 = slice(256 * n, 256 * n + 256)
            g[256 * b : 256 * b + 256, n4] = mm(left_side[...], right_side[:, n4]).astype(BF)

    def bias_grads():
        sums = jnp.sum(bsum[...], axis=0, keepdims=True)
        for n in range(10):
            bias[n : n + 1, :] = sums[:, 128 * n : 128 * n + 128]
        bias[10:16, :] = jnp.zeros((6, 128), F32)

    def local_rest(first, last):
        @pl.loop(first, last)
        def _(c):
            rows = ds256(c)
            embed[rows, :] = (mm(hid[rows, :], wo[...]) + bo[...]).astype(BF)
            total = jnp.zeros((256, 256), F32)
            for b in range(4):
                total = total + mm(da_t[b], dense[b, :, ds256(4 + c - b)])
            own[rows, :] = mm_t(dh[rows, :], ws[...]) + total.T

    def last_sum():
        for j in (0, 1, 2, 3):
            for m, dst in ((j, from_r), (4 + j, from_l)):
                remote(dst.at[j], dst.at[j], halo_send.at[8 + m], halo_recv.at[8 + m], left).wait_recv()
            rows = slice(256 * j, 256 * j + 256)
            outer = from_l[j].astype(F32) + from_r[j].astype(F32)
            gradf[rows, :] = (own[rows, :] + outer.T).astype(BF)

    loads[0].wait()
    build_dense()
    for c in loads[1:]:
        c.wait()
    local_part()
    for n in range(4):
        halo_wait(n)
    low_part()
    red = make_reduce(g, bias, gout, bout, *ar)
    for c in range(4):
        halo_wait(4 + c)
        if c < 3:
            chunk(c)
        else:
            chunk(c, 0, 128, 128)
            halo_wait(16)
            chunk(c, 128, 128, 256)
            weight_grad(0)
            red["pair"](0)
            weight_grad(1)
            red["pair"](1)
            red["over_first"](0)
        adjoint(c)
        adjoint_send(SENDS[c])
    weight_grad(2)
    red["pair"](2)
    red["over_first"](1)
    bias_grads()
    red["pair_bias"]()
    red["over_first"](2)
    red["bias_first"]()
    for stage in ("over_second", "over_z", "back_z", "back_second", "back_first"):
        before = red["started"]()
        for b in range(3):
            red[stage](b)
        adjoint_send(SENDS.get(stage, ()))
        if stage in REST:
            local_rest(*REST[stage])
            if REST[stage][1] == 4:
                write(embed, embed_hbm)
        tail = {"over_second": "bias_second", "over_z": "bias_z", "back_z": "bias_end"}.get(stage)
        if tail is not None:
            red[tail]()
        red["drain"](before)
    last_sum()
    write(gradf, gradf_hbm)
    before = red["started"]()
    red["back_pair"](0)
    red["back_pair"](1)
    red["back_end"](0)
    for n in range(4):
        n4 = slice(256 * n, 256 * n + 256)
        gwo[n4, :] = gout[0:256, n4].T
    write(gwo, gwo_hbm)
    red["back_pair"](2)
    red["drain"](before)
    red["back_end"](1)
    write(gout.at[pl.ds(256, 256), :], gws_hbm)
    red["back_end"](2)
    write(gout.at[pl.ds(512, 256), :], gwn_hbm)
    red["finish"]()
    for c in halo:
        c.wait_send()
    for c in writes:
        c.wait()


LAYER_SCRATCH = [
    pltpu.VMEM((1024, 256), BF),
    pltpu.VMEM((1024, 256), BF),
    pltpu.VMEM((768, 1024), BF),
    pltpu.VMEM((1024, 256), BF),
    pltpu.VMEM((3072, 256), BF),
    pltpu.VMEM((16, 64, 512), jnp.int32),
    pltpu.VMEM((256, 1024), BF),
    pltpu.VMEM((256, 1024), BF),
    pltpu.VMEM((1024, 256), BF),
    pltpu.VMEM((1024, 256), BF),
    pltpu.VMEM((8, 64, 128), F32),
    pltpu.VMEM((4, 256, 2304), BF),
    pltpu.VMEM((1024, 1024), F32),
    pltpu.VMEM((1024, 1024), F32),
    pltpu.VMEM((1024, 256), F32),
    pltpu.VMEM((256, 1024), BF),
    pltpu.VMEM((256, 1024), BF),
    pltpu.VMEM((256, 1024), BF),
    pltpu.VMEM((1024, 1024), BF),
    pltpu.VMEM((1024, 1024), BF),
    pltpu.VMEM((4, 256, 256), BF),
    pltpu.VMEM((8, 1280), F32),
    pltpu.VMEM((1024, 256), F32),
    pltpu.VMEM((256, 1024), F32),
    pltpu.VMEM((256, 1024), F32),
    pltpu.VMEM((4, 256, 256), BF),
    pltpu.VMEM((4, 256, 256), BF),
    pltpu.VMEM((4, 256, 256), BF),
    pltpu.VMEM((4, 256, 256), BF),
    pltpu.VMEM((768, 1024), BF),
    pltpu.VMEM((16, 128), F32),
    pltpu.SemaphoreType.DMA((6,)),
    pltpu.SemaphoreType.DMA((5,)),
    pltpu.SemaphoreType.DMA((17,)),
    pltpu.SemaphoreType.DMA((17,)),
]


def scale_kernel(embed, gradf, gws, gwn, bias, gwo, embed_o, gradf_o, gws_o, gwn_o, bh_o, gwo_o, bo_o):
    scale = 1.0 / math.sqrt(1024 * 256)
    embed_o[...] = embed[...]
    gradf_o[...] = gradf[...]
    gws_o[...] = gws[...].astype(F32) * scale
    gwn_o[...] = gwn[...].astype(F32) * scale
    gwo_o[...] = gwo[...].astype(F32) * scale
    bh_o[...] = bias[0:8, :] * scale
    bo_o[...] = bias[8:10, :] * scale


def scaled_outputs(embed, gradf, gws, gwn, bias, gwo):
    steps = 2
    tall = pl.BlockSpec((1024 // steps, 256), lambda i: (i, 0))
    wide = pl.BlockSpec((256 // steps, 1024), lambda i: (i, 0))

    def whole(rows):
        return pl.BlockSpec((rows, 128), lambda i: (0, 0))

    embed, gradf, gws, gwn, bh, gwo, bo = pl.pallas_call(
        scale_kernel,
        grid=(steps,),
        out_shape=(
            jax.ShapeDtypeStruct((1024, 256), BF),
            jax.ShapeDtypeStruct((1024, 256), BF),
            jax.ShapeDtypeStruct((256, 1024), F32),
            jax.ShapeDtypeStruct((256, 1024), F32),
            jax.ShapeDtypeStruct((8, 128), F32),
            jax.ShapeDtypeStruct((1024, 256), F32),
            jax.ShapeDtypeStruct((2, 128), F32),
        ),
        in_specs=[tall, tall, wide, wide, whole(16), tall],
        out_specs=(tall, tall, wide, wide, whole(8), tall, whole(2)),
        name="scaled_outputs",
    )(embed, gradf, gws, gwn, bias, gwo)
    return embed, gradf, gws, gwn, bh.reshape(1024), gwo, bo.reshape(256)


def local(
    node_features, tile_cols, tile_weights, w_self, w_neigh, bias_hidden, w_out, bias_out, cotangent
):
    vm = pl.BlockSpec(memory_space=pltpu.VMEM)
    hbm = pl.BlockSpec(memory_space=pl.ANY)
    sm = pl.BlockSpec(memory_space=pltpu.SMEM)
    embed, grad_features, gwo, gws, gwn, bias = pl.pallas_call(
        layer_kernel,
        out_shape=(
            jax.ShapeDtypeStruct((1024, 256), BF),
            jax.ShapeDtypeStruct((1024, 256), BF),
            jax.ShapeDtypeStruct((1024, 256), BF),
            jax.ShapeDtypeStruct((256, 1024), BF),
            jax.ShapeDtypeStruct((256, 1024), BF),
            jax.ShapeDtypeStruct((16, 128), F32),
        ),
        in_specs=[sm, hbm, hbm, hbm, hbm, vm, hbm, vm, hbm],
        out_specs=(hbm, hbm, hbm, hbm, hbm, vm),
        scratch_shapes=LAYER_SCRATCH + AR_SCRATCH,
        compiler_params=pltpu.CompilerParams(
            collective_id=0, has_side_effects=True, vmem_limit_bytes=60 << 20
        ),
        name="layer",
    )(
        tile_cols.T, node_features, tile_weights, w_self, w_neigh,
        bias_hidden.reshape(1, 1024), w_out, bias_out.reshape(1, 256), cotangent,
    )
    return scaled_outputs(embed, grad_features, gws, gwn, bias, gwo)


def solution(mesh):
    in_specs = (
        P(("row", "col"), None),
        P(("row", "col"), None),
        P(("row", "col"), None, None),
        P(),
        P(),
        P(),
        P(),
        P(),
        P(("row", "col"), None),
    )
    out_specs = (P(("row", "col"), None), P(("row", "col"), None), P(), P(), P(), P(), P())
    return jax.shard_map(local, mesh=mesh, in_specs=in_specs, out_specs=out_specs, check_vma=False)
```
